32 devices in a mesh: dp: 4 (over y, x), graph: 8 (over z, core).
Axes of the slice: x: 2, y: 2, z: 4, core: 2. Of those that a mesh axis runs over, the one named last changes fastest.
Arguments:
- nodes: bfloat16 [4, 128, 768], P('dp', 'graph'), may hold values from -6 to 6
- cotangent: bfloat16 [4, 128, 768], P('dp', 'graph'), may hold values from -16 to 16
- sources: int32 [4, 8192], P('dp', 'graph'), may hold values from 0 to 127
- targets: int32 [4, 8192], P('dp', 'graph'), may hold values from 0 to 127, as said below
- edge_weight: float32 [4, 8192], P('dp', 'graph'), may hold values from 0.2 to 1
- w_first: bfloat16 [1536, 768], replicated, may hold values from -0.15625 to 0.15625
- w_second: bfloat16 [768, 768], replicated, may hold values from -0.21875 to 0.21875
- biases: float32 [2, 768], replicated, may hold values from -3 to 3
- master: float32 [1769472], P(('dp', 'graph')), may hold values from -0.2 to 0.2
- moment_first: float32 [1769472], P(('dp', 'graph')), may hold values from -0.6 to 0.6
- moment_second: float32 [1769472], P(('dp', 'graph')), may hold values from 1 to 30
- bias_first: float32 [2, 768], replicated, may hold values from -12 to 12
- bias_second: float32 [2, 768], replicated, may hold values from 1 to 30
Outputs:
- node_out: bfloat16 [4, 128, 768], P('dp', 'graph')
- node_grad: float32 [4, 128, 768], P('dp', 'graph')
- new_master: float32 [1769472], P(('dp', 'graph'))
- new_first: float32 [1769472], P(('dp', 'graph'))
- new_second: float32 [1769472], P(('dp', 'graph'))
- new_biases: float32 [2, 768], replicated
- new_bias_first: float32 [2, 768], replicated
- new_bias_second: float32 [2, 768], replicated
The draws below stay inside these ranges and needn't reach their ends.
Inputs may be any that keep to these rules, and one draw needn't show every extreme that they name: `targets`: every node is the target of exactly 64 edges of its structure.
All inputs are finite; a program needn't handle non-finite values.
Results may differ from the reference program's by a relative error of at most 0.0031.
Values may be sent and summed in bfloat16 or wider, within the bound.
No kernel may reach another device: no remote copies, remote signals or barrier semaphores. Data moves between devices by JAX's collectives and lax.ppermute only.
A program may use at most 64 MiB of HBM per device.

```python
import math
import jax
import jax.numpy as jnp
from jax import lax

D = 768
NODE_DEV = 16
EDGE_DEV = 1024
STEP = 10
NODES = 128
EDGES = 8192
STRUCTS = 4
PARAMS = 1769472
N_DP = 4


def shuffle_row(row_key, owner_list):
    return jax.random.permutation(row_key, owner_list)


def draw_targets(key, part):
    degree = EDGES // NODES
    owner_list = jnp.arange(EDGES, dtype=jnp.int32) // degree
    row_keys = jax.random.split(jax.random.fold_in(key, 71), STRUCTS)
    shuffled = jax.vmap(shuffle_row, in_axes=(0, None))(row_keys, owner_list)
    return shuffled.astype(jnp.int32)


def draw_cotangent(key, part):
    inner = jax.random.fold_in(key, 113)
    flat_row = jnp.arange(STRUCTS * NODES, dtype=jnp.float32).reshape(STRUCTS, NODES, 1)
    rising = 10.0 ** (flat_row / (STRUCTS * NODES - 1.0)) / 4.0
    values = jnp.clip(jax.random.normal(inner, (STRUCTS, NODES, D), jnp.float32), -6.0, 6.0)
    return (values * rising).astype(jnp.bfloat16)


def with_ends(result, key, smallest, largest):
    index_at = [jax.random.randint(jax.random.fold_in(key, axis), (), 0, length) for axis, length in enumerate(result.shape)]
    main_axis = result.shape.index(max(result.shape))
    next_to = index_at[:main_axis] + [(index_at[main_axis] + 1) % result.shape[main_axis]] + index_at[main_axis + 1:]
    return result.at[tuple(index_at)].set(smallest).at[tuple(next_to)].set(largest)


def block_scale(stream_key, extent, shards, smallest, top_value):
    def one(dim, shards_of):
        heights = jax.random.uniform(jax.random.fold_in(jax.random.fold_in(stream_key, 6), dim), (shards_of,), jnp.float32, smallest / len(shards), top_value / len(shards))
        return jnp.repeat(jnp.exp(heights), extent[dim] // shards_of).reshape((-1,) + (1,) * (len(extent) - dim - 1))

    level = one(*shards[0])
    for cut in shards[1:]:
        level = level * one(*cut)
    return level


def scatter_about(stream_key, shape, spread, limit, shards=(), kind=jnp.bfloat16):
    values = spread * jax.random.normal(stream_key, shape, jnp.float32)
    if shards:
        values = values * block_scale(stream_key, shape, shards, -0.22, 0.18)
    return jnp.clip(values, -limit, limit).astype(kind)


def setup_inputs(seed: int = 0) -> dict:
    keys = jax.random.split(jax.random.key(seed), 14)
    return {
        "nodes": scatter_about(keys[0], (STRUCTS, NODES, D), 1.0, 6.0, ((0, 4), (1, 8))),
        "cotangent": draw_cotangent(jax.random.fold_in(keys[13], 71), 0),
        "sources": with_ends(jax.random.randint(keys[2], (STRUCTS, EDGES), 0, NODES), jax.random.fold_in(keys[2], 1), 0, NODES - 1).astype(jnp.int32),
        "targets": draw_targets(jax.random.fold_in(keys[13], 71), 0),
        "edge_weight": jnp.clip(jnp.exp(math.log(1.0) - 1.609438 * jax.random.uniform(keys[4], (STRUCTS, EDGES), jnp.float32) ** block_scale(keys[4], (STRUCTS, EDGES), ((0, 4), (1, 8)), -0.2, 0.2)), 0.2, 1.0),
        "w_first": scatter_about(keys[5], (2 * D, D), (2 * D) ** -0.5, 0.15625),
        "w_second": scatter_about(keys[6], (D, D), D ** -0.5, 0.21875),
        "biases": scatter_about(keys[7], (2, D), 0.5, 3.0, (), jnp.float32),
        "master": scatter_about(keys[8], (PARAMS,), 0.03, 0.2, ((0, 32),), jnp.float32),
        "moment_first": scatter_about(keys[9], (PARAMS,), 0.1, 0.6, ((0, 32),), jnp.float32),
        "moment_second": jnp.clip(jnp.exp(math.log(30.0) - 3.4011974 * jax.random.uniform(keys[10], (PARAMS,), jnp.float32) ** block_scale(keys[10], (PARAMS,), ((0, 32),), -0.2, 0.2)), 1.0, 30.0),
        "bias_first": scatter_about(keys[11], (2, D), 2.0, 12.0, (), jnp.float32),
        "bias_second": jnp.clip(jnp.exp(jax.random.uniform(keys[12], (2, D), jnp.float32, math.log(1.0), math.log(30.0))), 1.0, 30.0),
    }


beta_one = 0.9
beta_two = 0.999
epsilon = 1e-08
learn_rate = 0.001

def structure(nodes, cotangent, sources, targets, edge_weight, w_first, w_second, biases):
    norm_scale = 1.0 / math.sqrt(EDGE_DEV / NODE_DEV)
    envelope = edge_weight[:, None]
    from_rows = nodes[sources]
    to_rows = nodes[targets]
    preact = jnp.dot(from_rows, w_first[:D], preferred_element_type=jnp.float32) + jnp.dot(to_rows, w_first[D:], preferred_element_type=jnp.float32) + biases[0]
    activation = jax.nn.silu(preact).astype(jnp.bfloat16)
    message = ((jnp.dot(activation, w_second, preferred_element_type=jnp.float32) + biases[1]) * envelope).astype(jnp.bfloat16)
    summed = jax.ops.segment_sum(message.astype(jnp.float32), targets, num_segments=NODES)
    node_out = (nodes.astype(jnp.float32) + norm_scale * summed).astype(jnp.bfloat16)
    d_out = (cotangent[targets].astype(jnp.float32) * norm_scale * envelope).astype(jnp.bfloat16)
    grad_second = jnp.dot(activation.T, d_out, preferred_element_type=jnp.float32)
    d_act = jnp.dot(d_out, w_second.T, preferred_element_type=jnp.float32)
    sigmoid_pre = jax.nn.sigmoid(preact)
    d_pre = (d_act * sigmoid_pre * (1.0 + preact * (1.0 - sigmoid_pre))).astype(jnp.bfloat16)
    grad_first = jnp.concatenate([jnp.dot(from_rows.T, d_pre, preferred_element_type=jnp.float32), jnp.dot(to_rows.T, d_pre, preferred_element_type=jnp.float32)], 0)
    d_src = jnp.dot(d_pre, w_first[:D].T, preferred_element_type=jnp.float32).astype(jnp.bfloat16)
    d_dst = jnp.dot(d_pre, w_first[D:].T, preferred_element_type=jnp.float32).astype(jnp.bfloat16)
    node_part = jax.ops.segment_sum(d_src.astype(jnp.float32), sources, num_segments=NODES) + jax.ops.segment_sum(d_dst.astype(jnp.float32), targets, num_segments=NODES)
    node_grad = cotangent.astype(jnp.float32) + node_part
    flat_grads = jnp.concatenate([grad_first.reshape(-1), grad_second.reshape(-1)])
    bias_terms = jnp.stack([lax.optimization_barrier(jnp.sum(d_pre.astype(jnp.float32), 0)), lax.optimization_barrier(jnp.sum(d_out.astype(jnp.float32), 0))])
    return (node_out, node_grad, flat_grads, bias_terms)

def adam_update(param, first, second, grads):
    new_first = beta_one * first + (1.0 - beta_one) * grads
    new_second = beta_two * second + (1.0 - beta_two) * grads * grads
    ratio = new_first / (1.0 - beta_one ** STEP) / (jnp.sqrt(new_second / (1.0 - beta_two ** STEP)) + epsilon)
    return (param - learn_rate * ratio, new_first, new_second)

def reference(nodes, cotangent, sources, targets, edge_weight, w_first, w_second, biases, master, moment_first, moment_second, bias_first, bias_second):

    def one_struct(inputs):
        return structure(inputs[0], inputs[1], inputs[2], inputs[3], inputs[4], w_first, w_second, biases)
    node_out, node_grad, flat_grads, bias_terms = lax.map(one_struct, (nodes, cotangent, sources, targets, edge_weight))
    grads = lax.optimization_barrier(jnp.sum(flat_grads, 0)) / N_DP
    bias_grads = lax.optimization_barrier(jnp.sum(bias_terms, 0)) / N_DP
    new_master, new_first, new_second = adam_update(master, moment_first, moment_second, grads)
    new_biases, new_bias_first, new_bias_second = adam_update(biases, bias_first, bias_second, bias_grads)
    return (node_out, node_grad, new_master, new_first, new_second, new_biases, new_bias_first, new_bias_second)
```

```python
import functools
import math

import jax
import jax.numpy as jnp
from jax import lax
from jax.experimental import pallas as pl
from jax.experimental.pallas import tpu as pltpu
from jax.sharding import PartitionSpec as P

STEP = 10

beta_one = 0.9
beta_two = 0.999
epsilon = 1e-08
learn_rate = 0.001

F32 = jnp.float32
BF16 = jnp.bfloat16
LANES = 128
QUANTS = 8
DIGIT = 16.0

NN = (((1,), (0,)), ((), ()))
NT = (((1,), (1,)), ((), ()))


def dot(a, b, dims):
    return lax.dot_general(a, b, dims, preferred_element_type=F32)


def split_two(x):
    high = x.astype(BF16)
    low = (x - high.astype(F32)).astype(BF16)
    return high, low


def adam_update(param, first, second, grads):
    new_first = beta_one * first + (1.0 - beta_one) * grads
    new_second = beta_two * second + (1.0 - beta_two) * grads * grads
    ratio = (
        new_first
        / (1.0 - beta_one**STEP)
        / (jnp.sqrt(new_second / (1.0 - beta_two**STEP)) + epsilon)
    )
    return (param - learn_rate * ratio, new_first, new_second)


def pack_kernel(nodes_ref, cot_ref, src_ref, dst_ref, weight_ref, out_ref):
    rows, features = nodes_ref.shape
    width = out_ref.shape[1]
    beside = width - features
    rest = features - beside
    half = width - rest
    out_ref[:rows, :features] = nodes_ref[...]
    out_ref[:rows, features:] = cot_ref[:, :beside]
    out_ref[rows:, :rest] = cot_ref[:, beside:]

    def digits(ref):
        value = ref[...].astype(F32)
        high = jnp.floor(value * (1.0 / DIGIT))
        return high, value - high * DIGIT

    src_high, src_low = digits(src_ref)
    dst_high, dst_low = digits(dst_ref)
    weight = weight_ref[...]
    first = weight.astype(BF16).astype(F32)
    second = (weight - first).astype(BF16).astype(F32)
    third = weight - first - second
    quants = jnp.concatenate(
        [src_high, src_low, dst_high, dst_low, first, second, third, jnp.zeros_like(first)], 0
    )
    pieces = rows // QUANTS
    stacked = jnp.concatenate(
        [quants[:, i * half : (i + 1) * half] for i in range(pieces)], 0
    )
    out_ref[rows:, rest:] = stacked.astype(BF16)


def edge_kernel(scale, count, place_ref, *refs):
    blocks = refs[:count]
    first_ref, second_ref, bias_ref = refs[count : count + 3]
    sums_ref, envelope_ref, nodes_ref, cot_ref = refs[count + 3 : count + 7]
    window, left, edges, total = refs[count + 7 :]
    graph = place_ref[0]
    features = nodes_ref.shape[1]
    node_total = nodes_ref.shape[0]
    rows = node_total // count
    part = sums_ref.shape[0] // 3
    width = blocks[0].shape[1]
    beside = width - features
    rest = features - beside
    half = width - rest
    pieces = rows // QUANTS

    for k in range(count):
        at = pl.ds(pl.multiple_of((graph ^ k) * rows, rows), rows)
        nodes_ref[at, :] = blocks[k][:rows, :features]
        cot_ref[at, :beside] = blocks[k][:rows, features:]
        cot_ref[at, beside:] = blocks[k][rows:, :rest]
        quants = blocks[k][rows:, rest:].astype(F32)
        for i in range(pieces):
            edges[k, :, i * half : (i + 1) * half] = quants[i * QUANTS : (i + 1) * QUANTS]

    nodes = nodes_ref[...]
    cot = cot_ref[...]
    wide = first_ref.shape[1]
    offset = pl.multiple_of(place_ref[2], 8)
    mine = pl.ds(offset, part)
    window[...] = dot(nodes, first_ref[:features], NN).T
    src_part = window[mine, :]
    window[...] = (dot(nodes, first_ref[features:], NN) + bias_ref[:1, :]).T
    dst_part = window[mine, :]
    cot_part = dot(second_ref[...], cot, NT)
    del wide

    src_high, src_low = split_two(src_part)
    dst_high, dst_low = split_two(dst_part)
    cot_high, cot_low = split_two(cot_part)
    none = jnp.zeros_like(src_high)
    for i, (a, b) in enumerate(
        [(src_high, dst_high), (src_low, dst_low), (none, cot_high), (none, cot_low)]
    ):
        left[i * part : (i + 1) * part, :node_total] = a
        left[i * part : (i + 1) * part, node_total:] = b
    total[...] = jnp.zeros_like(total)
    edge_count = edges.shape[2]
    node_at = lax.broadcasted_iota(jnp.int32, (node_total, edge_count), 0).astype(F32)

    def body(k, carry):
        quants = edges[k]
        src = quants[0:1] * DIGIT + quants[1:2]
        dst = quants[2:3] * DIGIT + quants[3:4]
        weight = (quants[4:5] + quants[5:6] + quants[6:7]) * scale
        hot = jnp.concatenate(
            [
                jnp.where(node_at == src, 1.0, 0.0).astype(BF16),
                jnp.where(node_at == dst, 1.0, 0.0).astype(BF16),
            ],
            0,
        )
        got = dot(left[...], hot, NN)
        preact = got[:part] + got[part : 2 * part]
        d_act = (got[2 * part : 3 * part] + got[3 * part :]) * weight
        gate = 0.5 * jnp.tanh(0.5 * preact) + 0.5
        active = preact * gate
        d_pre = d_act * (gate + active * (1.0 - gate))
        high = weight.astype(BF16).astype(F32)
        low = weight - high
        tail = jnp.concatenate([high, low, jnp.zeros((14, edge_count), F32)], 0)
        right = jnp.concatenate(
            [(active * weight).astype(BF16), d_pre.astype(BF16), tail.astype(BF16)], 0
        )
        total[...] += dot(right, hot, NT)
        return carry

    lax.fori_loop(0, count, body, 0)
    sums_ref[:part] = total[:part, node_total:].astype(BF16)
    sums_ref[part : 2 * part] = total[part : 2 * part, :node_total].astype(BF16)
    sums_ref[2 * part :] = total[part : 2 * part, node_total:].astype(BF16)
    envelope = total[2 * part : 2 * part + 1, node_total:] + total[
        2 * part + 1 : 2 * part + 2, node_total:
    ]
    envelope_ref[...] = jnp.broadcast_to(envelope, envelope_ref.shape)


def take_rows(ref, start, rows):
    if rows % 8 == 0:
        return ref[pl.ds(pl.multiple_of(start, 8), rows), :]
    tall = row_window(rows)
    base = start // 8 * 8
    window = ref[pl.ds(pl.multiple_of(base, 8), tall), :]
    return pltpu.roll(window, lax.rem(tall - (start - base), tall), 0)[:rows]


def row_window(rows):
    return -(-rows // 8) * 8 + 8


def grad_kernel(count, groups, place_ref, *refs):
    blocks = refs[:count]
    nodes_ref, cot_ref, envelope_ref = refs[count : count + 3]
    outs = refs[count + 3 : count + 3 + groups]
    active_ref, src_ref, dst_ref = refs[count + 3 + groups : count + 6 + groups]
    left, src_sum, dst_sum = refs[count + 6 + groups :]
    graph, group = place_ref[0], place_ref[1]
    features = nodes_ref.shape[1]
    part = blocks[0].shape[0] // 3
    share = 3 * features // (groups * count)

    turned = nodes_ref[...].astype(F32).T
    left[:features] = turned
    left[features : 2 * features] = turned
    for k in range(count):
        start = pl.multiple_of((graph ^ k) * part, 8)
        block = blocks[k][...].astype(F32)
        left[pl.ds(pl.multiple_of(2 * features + start, 8), part), :] = block[:part]
        src_sum[pl.ds(start, part), :] = block[part : 2 * part]
        dst_sum[pl.ds(start, part), :] = block[2 * part :]

    src_all = src_sum[...].astype(BF16)
    dst_all = dst_sum[...].astype(BF16)
    cot = cot_ref[...]
    active_ref[...] = left[2 * features : 3 * features].astype(BF16)
    src_ref[...] = src_all
    dst_ref[...] = dst_all

    kinds = []
    rows = []
    for k in range(groups):
        start = (count * (group ^ k) + graph) * share
        rows.append(take_rows(left, start, share))
        kinds.append(start + lax.broadcasted_iota(jnp.int32, rows[-1].shape, 0))
    rows = jnp.concatenate(rows, 0)
    kinds = jnp.concatenate(kinds, 0)
    zero = jnp.zeros_like(rows)
    from_src = jnp.where(kinds < features, rows, zero).astype(BF16)
    from_dst = jnp.where((kinds >= features) & (kinds < 2 * features), rows, zero).astype(BF16)
    from_act = jnp.where(kinds >= 2 * features, rows, zero).astype(BF16)
    grads = dot(from_src, src_all, NT) + dot(from_dst, dst_all, NT) + dot(from_act, cot, NN)

    ones = jnp.ones((8, dst_all.shape[1]), BF16)
    bias_pre = dot(ones, dst_all, NT)[:1]
    env_high, env_low = split_two(envelope_ref[...])
    bias_out = (dot(env_high, cot, NN) + dot(env_low, cot, NN))[:1]
    pre_high = bias_pre.astype(BF16).astype(F32)
    out_high = bias_out.astype(BF16).astype(F32)
    tail = outs[0].shape[0] - share
    pad = jnp.zeros((tail - 4, features), F32)
    extra = jnp.concatenate(
        [pre_high, bias_pre - pre_high, out_high, bias_out - out_high, pad], 0
    )
    for k in range(groups):
        full = jnp.concatenate([grads[k * share : (k + 1) * share], extra], 0)
        outs[k][...] = full.astype(outs[k].dtype)


def node_kernel(place_ref, active_ref, src_ref, dst_ref, envelope_ref, first_ref, second_ref,
                bias_ref, nodes_ref, cot_ref, out_ref, grad_ref, wide):
    rows, features = nodes_ref.shape
    node_total = active_ref.shape[1]
    at = pl.ds(pl.multiple_of(place_ref[0] * rows, rows), rows)

    def own(ref):
        wide[...] = ref[...].astype(F32).T
        return wide[at, :].astype(BF16)

    active = own(active_ref)
    src = own(src_ref)
    dst = own(dst_ref)
    env = envelope_ref[...]
    column = jnp.broadcast_to(env[:1], (node_total, node_total)).T
    wide[:, :node_total] = column
    env_own = wide[at, :1]
    summed = dot(active, second_ref[...], NN) + env_own * bias_ref[1:2, :]
    out_ref[...] = (nodes_ref[...].astype(F32) + summed).astype(BF16)
    back = dot(src, first_ref[:features], NT) + dot(dst, first_ref[features:], NT)
    grad_ref[...] = cot_ref[...].astype(F32) + back


def adam_kernel(groups, *refs):
    parts = refs[:groups]
    master_ref, first_ref, second_ref, bias_ref, bias_first_ref, bias_second_ref = refs[
        groups : groups + 6
    ]
    outs = refs[groups + 6 : groups + 12]
    flat = refs[groups + 12]
    features = parts[0].shape[1]
    total = parts[0][...]
    for ref in parts[1:]:
        total = total + ref[...].astype(F32)
    total = total * (1.0 / groups)
    across = features // LANES
    share = flat.shape[0] // across
    for q in range(across):
        flat[pl.ds(q, share, stride=across), :] = total[:share, q * LANES : (q + 1) * LANES]
    results = adam_update(master_ref[...], first_ref[...], second_ref[...], flat[...])
    for ref, value in zip(outs[:3], results):
        ref[...] = value
    pairs = total[share : share + 4]
    bias_grads = jnp.concatenate([pairs[0:1] + pairs[1:2], pairs[2:3] + pairs[3:4]], 0)
    results = adam_update(bias_ref[...], bias_first_ref[...], bias_second_ref[...], bias_grads)
    for ref, value in zip(outs[3:], results):
        ref[...] = value


def swap(value, axis, count, distance):
    return lax.ppermute(value, axis, [(i, i ^ distance) for i in range(count)])


def gather_blocks(value, axis, count):
    far = {k: swap(value, axis, count, k) for k in range(count - 2, 0, -2)}
    blocks = {0: value, **far}
    for k in range(0, count, 2):
        blocks[k + 1] = swap(blocks[k], axis, count, 1)
    return [blocks[k] for k in range(count)]


def smem():
    return pl.BlockSpec(memory_space=pltpu.SMEM)


def vmem(n):
    return [pl.BlockSpec(memory_space=pltpu.VMEM)] * n


def call(body, ins, outs, scratch=(), place=None, flops=0):
    arrays = list(ins)
    specs = vmem(len(arrays))
    if place is not None:
        arrays = [place] + arrays
        specs = [smem()] + specs
    moved = sum(a.size * a.dtype.itemsize for a in list(ins) + list(outs))
    return pl.pallas_call(
        body,
        out_shape=tuple(outs),
        in_specs=specs,
        out_specs=tuple(vmem(len(outs))),
        scratch_shapes=list(scratch),
        cost_estimate=pl.CostEstimate(flops=flops, bytes_accessed=moved, transcendentals=0),
    )(*arrays)


def shards(
    nodes,
    cotangent,
    sources,
    targets,
    edge_weight,
    w_first,
    w_second,
    biases,
    master,
    moment_first,
    moment_second,
    bias_first,
    bias_second,
):
    features = nodes.shape[2]
    rows = nodes.shape[1]
    edge_count = sources.shape[1]
    scale = 1.0 / math.sqrt(edge_count / rows)
    count = lax.axis_size("graph")
    groups = lax.axis_size("dp")
    node_total = rows * count
    part = features // count
    share = master.shape[0] // features
    struct = jax.ShapeDtypeStruct
    graph = lax.axis_index("graph")
    group = lax.axis_index("dp")

    wide = min(features, 2 * LANES)
    begin = jnp.minimum(graph * part // LANES * LANES, features - wide)
    place = jnp.stack([graph, group, graph * part - begin]).astype(jnp.int32)
    first_part = lax.dynamic_slice(w_first, (0, begin), (2 * features, wide))
    second_part = lax.dynamic_slice(w_second, (graph * part, 0), (part, features))
    bias_part = lax.dynamic_slice(biases, (0, begin), (2, wide))

    width = max(features, edge_count)
    (packed,) = call(
        pack_kernel,
        [nodes[0], cotangent[0], sources, targets, edge_weight],
        [struct((2 * rows, width), BF16)],
    )
    blocks = gather_blocks(packed, "graph", count)
    sums, envelope, all_nodes, all_cot = call(
        functools.partial(edge_kernel, scale, count),
        blocks + [first_part, second_part, bias_part],
        [
            struct((3 * part, node_total), BF16),
            struct((8, node_total), F32),
            struct((node_total, features), BF16),
            struct((node_total, features), BF16),
        ],
        [
            pltpu.VMEM((wide, node_total), F32),
            pltpu.VMEM((4 * part, 2 * node_total), BF16),
            pltpu.VMEM((count, QUANTS, edge_count), F32),
            pltpu.VMEM((2 * part + 16, 2 * node_total), F32),
        ],
        place=place,
        flops=8 * part * 2 * node_total * edge_count * count,
    )
    blocks = gather_blocks(sums, "graph", count)
    tall = -(-(share + 4) // 16) * 16
    results = call(
        functools.partial(grad_kernel, count, groups),
        blocks + [all_nodes, all_cot, envelope],
        [struct((tall, features), F32)]
        + [struct((tall, features), BF16)] * (groups - 1)
        + [struct((features, node_total), BF16)] * 3,
        [
            pltpu.VMEM((3 * features + 16, node_total), F32),
            pltpu.VMEM((features, node_total), F32),
            pltpu.VMEM((features, node_total), F32),
        ],
        place=place,
        flops=2 * groups * share * 3 * node_total * features,
    )
    grads = results[:groups]
    active, src_sum, dst_sum = results[groups:]
    received = [grads[0]] + [swap(grads[k], "dp", groups, k) for k in range(1, groups)]
    node_out, node_grad = call(
        node_kernel,
        [active, src_sum, dst_sum, envelope, w_first, w_second, biases, nodes[0], cotangent[0]],
        [struct((rows, features), BF16), struct((rows, features), F32)],
        [pltpu.VMEM((node_total, features), F32)],
        place=place,
        flops=6 * node_total * features * features,
    )
    lanes = (share * (features // LANES), LANES)
    updated = call(
        functools.partial(adam_kernel, groups),
        received
        + [master.reshape(lanes), moment_first.reshape(lanes), moment_second.reshape(lanes)]
        + [biases, bias_first, bias_second],
        [struct(lanes, F32)] * 3 + [struct(biases.shape, F32)] * 3,
        [pltpu.VMEM(lanes, F32)],
    )
    return (
        node_out[None],
        node_grad[None],
        updated[0].reshape(master.shape),
        updated[1].reshape(master.shape),
        updated[2].reshape(master.shape),
        updated[3],
        updated[4],
        updated[5],
    )


def solution(mesh):
    placed = (
        P("dp", "graph", None),
        P("dp", "graph", None),
        P("dp", "graph"),
        P("dp", "graph"),
        P("dp", "graph"),
        P(),
        P(),
        P(),
        P(("dp", "graph")),
        P(("dp", "graph")),
        P(("dp", "graph")),
        P(),
        P(),
    )
    return jax.shard_map(
        shards,
        mesh=mesh,
        in_specs=placed,
        out_specs=(
            P("dp", "graph", None),
            P("dp", "graph", None),
            P(("dp", "graph")),
            P(("dp", "graph")),
            P(("dp", "graph")),
            P(),
            P(),
            P(),
        ),
        check_vma=False,
    )
```

```python
import functools
import math

import jax
import jax.numpy as jnp
from jax import lax
from jax.experimental import pallas as pl
from jax.experimental.pallas import tpu as pltpu
from jax.sharding import PartitionSpec as P

STEP = 10

beta_one = 0.9
beta_two = 0.999
epsilon = 1e-08
learn_rate = 0.001

F32 = jnp.float32
BF16 = jnp.bfloat16
LANES = 128
EXACT = 256
DIGIT = 16.0

NN = (((1,), (0,)), ((), ()))
NT = (((1,), (1,)), ((), ()))


def dot(a, b, dims):
    return lax.dot_general(a, b, dims, preferred_element_type=F32)


def split_two(x):
    high = x.astype(BF16)
    low = (x - high.astype(F32)).astype(BF16)
    return high, low


def adam_update(param, first, second, grads):
    new_first = beta_one * first + (1.0 - beta_one) * grads
    new_second = beta_two * second + (1.0 - beta_two) * grads * grads
    ratio = (
        new_first
        / (1.0 - beta_one**STEP)
        / (jnp.sqrt(new_second / (1.0 - beta_two**STEP)) + epsilon)
    )
    return (param - learn_rate * ratio, new_first, new_second)


def pack_kernel(quants, *refs):
    sources, out_ref, held, sems = refs[:5], refs[5], refs[6:11], refs[11]
    copies = [
        pltpu.make_async_copy(source, target, sems.at[i])
        for i, (source, target) in enumerate(zip(sources, held))
    ]
    for copy in copies:
        copy.start()
    for copy in copies:
        copy.wait()
    nodes_ref, cot_ref, src_ref, dst_ref, weight_ref = held
    rows, features = nodes_ref.shape
    width = out_ref.shape[1]
    beside = width - features
    rest = features - beside
    half = width - rest
    out_ref[:rows, :features] = nodes_ref[...]
    out_ref[:rows, features:] = cot_ref[:, :beside]
    out_ref[rows:, :rest] = cot_ref[:, beside:]

    src = src_ref[...].astype(F32)
    dst = dst_ref[...].astype(F32)
    weight = weight_ref[...]
    first = weight.astype(BF16).astype(F32)
    second = (weight - first).astype(BF16).astype(F32)
    if quants == 4:
        values = [src, dst, first, second]
    else:
        src_high = jnp.floor(src * (1.0 / DIGIT))
        dst_high = jnp.floor(dst * (1.0 / DIGIT))
        values = [src_high, src - src_high * DIGIT, dst_high, dst - dst_high * DIGIT]
        values += [first, second, weight - first - second, jnp.zeros_like(first)]
    values = jnp.concatenate(values, 0)
    pieces = rows // quants
    stacked = jnp.concatenate(
        [values[:, i * half : (i + 1) * half] for i in range(pieces)], 0
    )
    out_ref[rows:, rest:] = stacked.astype(BF16)


def weight_kernel(split, place_ref, first_ref, second_ref, bias_ref, first_out, second_out, bias_out,
                  held, second_held, bias_held, turned, sems):
    features, part = second_ref.shape[1], second_out.shape[0]
    wide, tall = held.shape[1], second_held.shape[0]
    column = lax.rem(place_ref[0], split) * part
    begin = pl.multiple_of(jnp.minimum(column // LANES * LANES, features - wide), LANES)
    high = pl.multiple_of(jnp.minimum(column // 16 * 16, features - tall), 16)
    columns = pl.ds(begin, wide)
    copies = [
        pltpu.make_async_copy(first_ref.at[:, columns], held, sems.at[0]),
        pltpu.make_async_copy(second_ref.at[pl.ds(high, tall), :], second_held, sems.at[1]),
        pltpu.make_async_copy(bias_ref.at[:, columns], bias_held, sems.at[2]),
    ]
    for copy in copies:
        copy.start()
    for copy in copies:
        copy.wait()
    mine = pl.ds(pl.multiple_of(column - begin, 8), part)
    for i in range(2):
        turned[...] = held[i * features : (i + 1) * features].astype(F32).T
        first_out[i] = turned[mine, :].astype(BF16)
    turned[:, :LANES] = jnp.broadcast_to(bias_held[:1, :], (LANES, wide)).T
    bias_out[...] = turned[mine, :LANES]
    turned[:tall, :] = second_held[...].astype(F32)
    second_out[...] = turned[pl.ds(pl.multiple_of(column - high, 8), part), :].astype(BF16)


def edge_kernel(scale, count, place_ref, *refs):
    blocks = refs[:count]
    first_ref, second_ref, bias_ref = refs[count : count + 3]
    sums_ref, envelope_ref, nodes_ref, cot_ref = refs[count + 3 : count + 7]
    left, left_back, edges, total = refs[count + 7 :]
    graph = place_ref[0]
    features = nodes_ref.shape[1]
    node_total = nodes_ref.shape[0]
    rows = node_total // count
    part = sums_ref.shape[0] // 3
    width = blocks[0].shape[1]
    beside = width - features
    rest = features - beside
    half = width - rest
    quants = edges.shape[1]
    pieces = rows // quants

    for k in range(count):
        at = pl.ds(pl.multiple_of((graph ^ k) * rows, rows), rows)
        nodes_ref[at, :] = blocks[k][:rows, :features]
        cot_ref[at, :beside] = blocks[k][:rows, features:]
        cot_ref[at, beside:] = blocks[k][rows:, :rest]
        numbers = blocks[k][rows:, rest:].astype(F32)
        for i in range(pieces):
            edges[k, :, i * half : (i + 1) * half] = numbers[i * quants : (i + 1) * quants]

    nodes = nodes_ref[...]
    cot = cot_ref[...]
    src_part = dot(first_ref[0], nodes, NT)
    dst_part = dot(first_ref[1], nodes, NT) + bias_ref[:, :1]
    cot_part = dot(second_ref[...], cot, NT)

    src_high, src_low = split_two(0.5 * src_part)
    dst_high, dst_low = split_two(0.5 * dst_part)
    cot_high, cot_low = split_two((0.5 * scale) * cot_part)
    for i, piece in enumerate([src_high, dst_high, src_low, dst_low]):
        left[:, i * node_total : (i + 1) * node_total] = piece
    left_back[:, :node_total] = cot_high
    left_back[:, node_total:] = cot_low
    total[...] = jnp.zeros_like(total)
    kind = BF16 if quants == 4 else F32
    step = edges.shape[2]
    node_at = lax.broadcasted_iota(jnp.int32, (node_total, step), 0).astype(F32).astype(kind)

    def one_hot(row):
        same = node_at == row.astype(kind)
        return jnp.where(same, jnp.ones((), kind), jnp.zeros((), kind)).astype(BF16)

    def body(k, carry):
        numbers = edges[k]
        if quants == 4:
            src, dst = numbers[0:1], numbers[1:2]
            weight = numbers[2:3] + numbers[3:4]
        else:
            src = numbers[0:1] * DIGIT + numbers[1:2]
            dst = numbers[2:3] * DIGIT + numbers[3:4]
            weight = numbers[4:5] + numbers[5:6] + numbers[6:7]
        src_hot, dst_hot = one_hot(src), one_hot(dst)
        hot = jnp.concatenate([src_hot, dst_hot], 0)
        halved = dot(left[...], jnp.concatenate([hot, hot], 0), NN)
        back = dot(left_back[...], jnp.concatenate([dst_hot, dst_hot], 0), NN) * weight
        tilt = jnp.tanh(halved)
        rise = 1.0 + tilt
        active = (halved * rise) * weight
        d_pre = back * (rise * (1.0 + halved * (1.0 - tilt)))
        high = weight.astype(BF16).astype(F32)
        low = weight - high
        tail = jnp.concatenate([high, low, jnp.zeros((14, step), F32)], 0)
        right = jnp.concatenate(
            [active.astype(BF16), d_pre.astype(BF16), tail.astype(BF16)], 0
        )
        total[...] += dot(right, hot, NT)
        return carry

    lax.fori_loop(0, edges.shape[0], body, 0, unroll=8)
    sums_ref[:part] = (scale * total[:part, node_total:]).astype(BF16)
    sums_ref[part : 2 * part] = total[part : 2 * part, :node_total].astype(BF16)
    sums_ref[2 * part :] = total[part : 2 * part, node_total:].astype(BF16)
    envelope = scale * (
        total[2 * part : 2 * part + 1, node_total:]
        + total[2 * part + 1 : 2 * part + 2, node_total:]
    )
    envelope_ref[...] = jnp.broadcast_to(envelope, envelope_ref.shape)


def take_rows(ref, start, rows):
    if rows % 8 == 0:
        return ref[pl.ds(pl.multiple_of(start, 8), rows), :]
    tall = row_window(rows)
    base = start // 8 * 8
    window = ref[pl.ds(pl.multiple_of(base, 8), tall), :]
    return pltpu.roll(window, lax.rem(tall - (start - base), tall), 0)[:rows]


def row_window(rows):
    return -(-rows // 8) * 8 + 8


def grad_kernel(split, count, groups, place_ref, *refs):
    blocks = refs[:split]
    nodes_ref, cot_ref, envelope_ref = refs[split : split + 3]
    outs = refs[split + 3 : split + 3 + groups]
    active_ref, src_ref, dst_ref = refs[split + 3 + groups : split + 6 + groups]
    left, src_sum, dst_sum = refs[split + 6 + groups :]
    graph, group = place_ref[0], place_ref[1]
    features = nodes_ref.shape[1]
    part = blocks[0].shape[0] // 3
    share = 3 * features // (groups * count)

    turned = nodes_ref[...].astype(F32).T
    left[:features] = turned
    left[features : 2 * features] = turned
    slot = lax.rem(graph, split)
    for k in range(split):
        start = pl.multiple_of((slot ^ k) * part, 8)
        block = blocks[k][...].astype(F32)
        left[pl.ds(pl.multiple_of(2 * features + start, 8), part), :] = block[:part]
        src_sum[pl.ds(start, part), :] = block[part : 2 * part]
        dst_sum[pl.ds(start, part), :] = block[2 * part :]

    src_all = src_sum[...].astype(BF16)
    dst_all = dst_sum[...].astype(BF16)
    cot = cot_ref[...]
    active_ref[...] = left[2 * features : 3 * features].astype(BF16)
    src_ref[...] = src_all
    dst_ref[...] = dst_all

    kinds = []
    rows = []
    for k in range(groups):
        start = (count * (group ^ k) + graph) * share
        rows.append(take_rows(left, start, share))
        kinds.append(start + lax.broadcasted_iota(jnp.int32, rows[-1].shape, 0))
    rows = jnp.concatenate(rows, 0)
    kinds = jnp.concatenate(kinds, 0)
    zero = jnp.zeros_like(rows)
    from_src = jnp.where(kinds < features, rows, zero).astype(BF16)
    from_dst = jnp.where((kinds >= features) & (kinds < 2 * features), rows, zero).astype(BF16)
    from_act = jnp.where(kinds >= 2 * features, rows, zero).astype(BF16)
    grads = dot(from_src, src_all, NT) + dot(from_dst, dst_all, NT) + dot(from_act, cot, NN)

    ones = jnp.ones((8, dst_all.shape[1]), BF16)
    bias_pre = dot(ones, dst_all, NT)[:1]
    env_high, env_low = split_two(envelope_ref[...])
    bias_out = (dot(env_high, cot, NN) + dot(env_low, cot, NN))[:1]
    pre_high = bias_pre.astype(BF16).astype(F32)
    out_high = bias_out.astype(BF16).astype(F32)
    tail = outs[0].shape[0] - share
    pad = jnp.zeros((tail - 4, features), F32)
    extra = jnp.concatenate(
        [pre_high, bias_pre - pre_high, out_high, bias_out - out_high, pad], 0
    )
    for k in range(groups):
        full = jnp.concatenate([grads[k * share : (k + 1) * share], extra], 0)
        outs[k][...] = full.astype(outs[k].dtype)


def node_kernel(place_ref, active_ref, src_ref, dst_ref, envelope_ref, first_ref, second_ref,
                bias_ref, nodes_ref, cot_ref, out_ref, grad_ref, wide):
    rows, features = nodes_ref.shape
    node_total = active_ref.shape[1]
    at = pl.ds(pl.multiple_of(place_ref[0] * rows, rows), rows)

    def own(ref):
        wide[...] = ref[...].astype(F32).T
        return wide[at, :].astype(BF16)

    active = own(active_ref)
    src = own(src_ref)
    dst = own(dst_ref)
    env = envelope_ref[...]
    column = jnp.broadcast_to(env[:1], (node_total, node_total)).T
    wide[:, :node_total] = column
    env_own = wide[at, :1]
    summed = dot(active, second_ref[...], NN) + env_own * bias_ref[1:2, :]
    out_ref[...] = (nodes_ref[...].astype(F32) + summed).astype(BF16)
    back = dot(src, first_ref[:features], NT) + dot(dst, first_ref[features:], NT)
    grad_ref[...] = cot_ref[...].astype(F32) + back


def adam_kernel(groups, *refs):
    parts = refs[:groups]
    master_ref, first_ref, second_ref, bias_ref, bias_first_ref, bias_second_ref = refs[
        groups : groups + 6
    ]
    outs = refs[groups + 6 : groups + 12]
    flat = refs[groups + 12]
    features = parts[0].shape[1]
    total = parts[0][...]
    for ref in parts[1:]:
        total = total + ref[...].astype(F32)
    total = total * (1.0 / groups)
    across = features // LANES
    share = flat.shape[0] // across
    for q in range(across):
        flat[pl.ds(q, share, stride=across), :] = total[:share, q * LANES : (q + 1) * LANES]
    results = adam_update(master_ref[...], first_ref[...], second_ref[...], flat[...])
    for ref, value in zip(outs[:3], results):
        ref[...] = value
    pairs = total[share : share + 4]
    bias_grads = jnp.concatenate([pairs[0:1] + pairs[1:2], pairs[2:3] + pairs[3:4]], 0)
    results = adam_update(bias_ref[...], bias_first_ref[...], bias_second_ref[...], bias_grads)
    for ref, value in zip(outs[3:], results):
        ref[...] = value


def swap(value, axis, count, distance):
    return lax.ppermute(value, axis, [(i, i ^ distance) for i in range(count)])


def gather_blocks(value, axis, count, reach):
    far = {k: swap(value, axis, count, k) for k in range(reach - 2, 0, -2)}
    blocks = {0: value, **far}
    for k in range(0, reach, 2):
        blocks[k + 1] = swap(blocks[k], axis, count, 1)
    return [blocks[k] for k in range(reach)]


def smem():
    return pl.BlockSpec(memory_space=pltpu.SMEM)


def call(body, ins, outs, scratch=(), place=None, flops=0, room=24 << 20,
         far=()):
    far = set(far)
    arrays = [
        pltpu.with_memory_space_constraint(a, pltpu.HBM) if i in far else a
        for i, a in enumerate(ins)
    ]
    specs = [
        pl.BlockSpec(memory_space=pltpu.HBM if i in far else pltpu.VMEM)
        for i in range(len(arrays))
    ]
    if place is not None:
        arrays = [place] + arrays
        specs = [smem()] + specs
    moved = sum(a.size * a.dtype.itemsize for a in list(ins) + list(outs))
    return pl.pallas_call(
        body,
        out_shape=tuple(outs),
        in_specs=specs,
        out_specs=tuple([pl.BlockSpec(memory_space=pltpu.VMEM)] * len(outs)),
        scratch_shapes=list(scratch),
        compiler_params=pltpu.CompilerParams(vmem_limit_bytes=room),
        cost_estimate=pl.CostEstimate(flops=flops, bytes_accessed=moved, transcendentals=0),
    )(*arrays)


def shards(
    nodes,
    cotangent,
    sources,
    targets,
    edge_weight,
    w_first,
    w_second,
    biases,
    master,
    moment_first,
    moment_second,
    bias_first,
    bias_second,
):
    features = nodes.shape[2]
    rows = nodes.shape[1]
    edge_count = sources.shape[1]
    scale = 1.0 / math.sqrt(edge_count / rows)
    count = lax.axis_size("graph")
    groups = lax.axis_size("dp")
    node_total = rows * count
    split = min(count, 4)
    part = features // split
    share = master.shape[0] // features
    struct = jax.ShapeDtypeStruct
    graph = lax.axis_index("graph")
    group = lax.axis_index("dp")

    over = max(i * part % LANES for i in range(split))
    wide = min(features, -(-(part + over) // LANES) * LANES)
    tall = min(features, part if part % 16 == 0 else -(-part // 16) * 16 + 16)
    place = jnp.stack([graph, group]).astype(jnp.int32)

    quants = 4 if node_total <= EXACT else 8
    width = features + quants * edge_count // (2 * rows)
    sources_in = [nodes[0], cotangent[0], sources, targets, edge_weight]
    (packed,) = call(
        functools.partial(pack_kernel, quants),
        sources_in,
        [struct((2 * rows, width), BF16)],
        [pltpu.VMEM(a.shape, a.dtype) for a in sources_in]
        + [pltpu.SemaphoreType.DMA((len(sources_in),))],
        far=range(len(sources_in)),
    )
    blocks = gather_blocks(packed, "graph", count, count)
    weights = call(
        functools.partial(weight_kernel, split),
        [w_first, w_second, biases],
        [
            struct((2, part, features), BF16),
            struct((part, features), BF16),
            struct((part, LANES), F32),
        ],
        [
            pltpu.VMEM((2 * features, wide), BF16),
            pltpu.VMEM((tall, features), BF16),
            pltpu.VMEM((2, wide), F32),
            pltpu.VMEM((wide, features), F32),
            pltpu.SemaphoreType.DMA((3,)),
        ],
        place=place,
        far=range(3),
    )
    sums, envelope, all_nodes, all_cot = call(
        functools.partial(edge_kernel, scale, count),
        blocks + list(weights),
        [
            struct((3 * part, node_total), BF16),
            struct((8, node_total), F32),
            struct((node_total, features), BF16),
            struct((node_total, features), BF16),
        ],
        [
            pltpu.VMEM((part, 4 * node_total), BF16),
            pltpu.VMEM((part, 2 * node_total), BF16),
            pltpu.VMEM((count, quants, edge_count), F32),
            pltpu.VMEM((2 * part + 16, 2 * node_total), F32),
        ],
        place=place,
        flops=8 * part * 2 * node_total * edge_count * count,
    )
    blocks = gather_blocks(sums, "graph", count, split)
    tall = -(-(share + 4) // 16) * 16
    results = call(
        functools.partial(grad_kernel, split, count, groups),
        blocks + [all_nodes, all_cot, envelope],
        [struct((tall, features), F32)]
        + [struct((tall, features), BF16)] * (groups - 1)
        + [struct((features, node_total), BF16)] * 3,
        [
            pltpu.VMEM((3 * features + 16, node_total), F32),
            pltpu.VMEM((features, node_total), F32),
            pltpu.VMEM((features, node_total), F32),
        ],
        place=place,
        flops=2 * groups * share * 3 * node_total * features,
    )
    grads = results[:groups]
    active, src_sum, dst_sum = results[groups:]
    received = [grads[0]] + [swap(grads[k], "dp", groups, k) for k in range(1, groups)]
    node_out, node_grad = call(
        node_kernel,
        [active, src_sum, dst_sum, envelope, w_first, w_second, biases, nodes[0], cotangent[0]],
        [struct((rows, features), BF16), struct((rows, features), F32)],
        [pltpu.VMEM((node_total, features), F32)],
        place=place,
        flops=6 * node_total * features * features,
    )
    lanes = (share * (features // LANES), LANES)
    updated = call(
        functools.partial(adam_kernel, groups),
        received
        + [master.reshape(lanes), moment_first.reshape(lanes), moment_second.reshape(lanes)]
        + [biases, bias_first, bias_second],
        [struct(lanes, F32)] * 3 + [struct(biases.shape, F32)] * 3,
        [pltpu.VMEM(lanes, F32)],
    )
    return (
        node_out[None],
        node_grad[None],
        updated[0].reshape(master.shape),
        updated[1].reshape(master.shape),
        updated[2].reshape(master.shape),
        updated[3],
        updated[4],
        updated[5],
    )


def solution(mesh):
    placed = (
        P("dp", "graph", None),
        P("dp", "graph", None),
        P("dp", "graph"),
        P("dp", "graph"),
        P("dp", "graph"),
        P(),
        P(),
        P(),
        P(("dp", "graph")),
        P(("dp", "graph")),
        P(("dp", "graph")),
        P(),
        P(),
    )
    return jax.shard_map(
        shards,
        mesh=mesh,
        in_specs=placed,
        out_specs=(
            P("dp", "graph", None),
            P("dp", "graph", None),
            P(("dp", "graph")),
            P(("dp", "graph")),
            P(("dp", "graph")),
            P(),
            P(),
            P(),
        ),
        check_vma=False,
    )
```

```python
import functools
import math

import jax
import jax.numpy as jnp
from jax import lax
from jax.experimental import pallas as pl
from jax.experimental.pallas import tpu as pltpu
from jax.sharding import PartitionSpec as P


STEP = 10

beta_one = 0.9
beta_two = 0.999
epsilon = 1e-08
learn_rate = 0.001

F32 = jnp.float32
BF16 = jnp.bfloat16
LANES = 128
EXACT = 256
DIGIT = 16.0

NN = (((1,), (0,)), ((), ()))
NT = (((1,), (1,)), ((), ()))


def dot(a, b, dims):
    return lax.dot_general(a, b, dims, preferred_element_type=F32)


def split_two(x):
    high = x.astype(BF16)
    low = (x - high.astype(F32)).astype(BF16)
    return high, low


def adam_update(param, first, second, grads):
    new_first = beta_one * first + (1.0 - beta_one) * grads
    new_second = beta_two * second + (1.0 - beta_two) * grads * grads
    ratio = (
        new_first
        / (1.0 - beta_one**STEP)
        / (jnp.sqrt(new_second / (1.0 - beta_two**STEP)) + epsilon)
    )
    return (param - learn_rate * ratio, new_first, new_second)


def pack_kernel(quants, *refs):
    sources, out_ref, held, sems = refs[:5], refs[5], refs[6:11], refs[11]
    copies = [
        pltpu.make_async_copy(source, target, sems.at[i])
        for i, (source, target) in enumerate(zip(sources, held))
    ]
    for copy in copies:
        copy.start()
    for copy in copies:
        copy.wait()
    nodes_ref, cot_ref, src_ref, dst_ref, weight_ref = held
    rows, features = nodes_ref.shape
    width = out_ref.shape[1]
    beside = width - features
    rest = features - beside
    half = width - rest
    out_ref[:rows, :features] = nodes_ref[...]
    out_ref[:rows, features:] = cot_ref[:, :beside]
    out_ref[rows:, :rest] = cot_ref[:, beside:]

    src = src_ref[...].astype(F32)
    dst = dst_ref[...].astype(F32)
    weight = weight_ref[...]
    first = weight.astype(BF16).astype(F32)
    second = (weight - first).astype(BF16).astype(F32)
    if quants == 4:
        values = [src, dst, first, second]
    else:
        src_high = jnp.floor(src * (1.0 / DIGIT))
        dst_high = jnp.floor(dst * (1.0 / DIGIT))
        values = [src_high, src - src_high * DIGIT, dst_high, dst - dst_high * DIGIT]
        values += [first, second, weight - first - second, jnp.zeros_like(first)]
    values = jnp.concatenate(values, 0)
    pieces = rows // quants
    stacked = jnp.concatenate(
        [values[:, i * half : (i + 1) * half] for i in range(pieces)], 0
    )
    out_ref[rows:, rest:] = stacked.astype(BF16)


def weight_kernel(split, place_ref, first_ref, second_ref, bias_ref, first_out, second_out, bias_out,
                  held, second_held, bias_held, turned, sems):
    features, part = second_ref.shape[1], second_out.shape[0]
    wide, tall = held.shape[1], second_held.shape[0]
    column = lax.rem(place_ref[0], split) * part
    begin = pl.multiple_of(jnp.minimum(column // LANES * LANES, features - wide), LANES)
    high = pl.multiple_of(jnp.minimum(column // 16 * 16, features - tall), 16)
    columns = pl.ds(begin, wide)
    copies = [
        pltpu.make_async_copy(first_ref.at[:, columns], held, sems.at[0]),
        pltpu.make_async_copy(second_ref.at[pl.ds(high, tall), :], second_held, sems.at[1]),
        pltpu.make_async_copy(bias_ref.at[:, columns], bias_held, sems.at[2]),
    ]
    for copy in copies:
        copy.start()
    for copy in copies:
        copy.wait()
    mine = pl.ds(pl.multiple_of(column - begin, 8), part)
    for i in range(2):
        turned[...] = held[i * features : (i + 1) * features].astype(F32).T
        first_out[i] = turned[mine, :].astype(BF16)
    turned[:, :LANES] = jnp.broadcast_to(bias_held[:1, :], (LANES, wide)).T
    bias_out[...] = turned[mine, :LANES]
    turned[:tall, :] = second_held[...].astype(F32)
    second_out[...] = turned[pl.ds(pl.multiple_of(column - high, 8), part), :].astype(BF16)


def edge_kernel(scale, count, place_ref, *refs):
    blocks = refs[:count]
    first_ref, second_ref, bias_ref = refs[count : count + 3]
    sums_ref, envelope_ref, nodes_ref, cot_ref = refs[count + 3 : count + 7]
    left, left_back, edges, total = refs[count + 7 :]
    graph = place_ref[0]
    features = nodes_ref.shape[1]
    node_total = nodes_ref.shape[0]
    rows = node_total // count
    part = sums_ref.shape[0] // 3
    width = blocks[0].shape[1]
    beside = width - features
    rest = features - beside
    half = width - rest
    quants = edges.shape[1]
    pieces = rows // quants

    for k in range(count):
        at = pl.ds(pl.multiple_of((graph ^ k) * rows, rows), rows)
        nodes_ref[at, :] = blocks[k][:rows, :features]
        cot_ref[at, :beside] = blocks[k][:rows, features:]
        cot_ref[at, beside:] = blocks[k][rows:, :rest]
        numbers = blocks[k][rows:, rest:].astype(F32)
        for i in range(pieces):
            edges[k, :, i * half : (i + 1) * half] = numbers[i * quants : (i + 1) * quants]

    nodes = nodes_ref[...]
    cot = cot_ref[...]
    src_part = dot(first_ref[0], nodes, NT)
    dst_part = dot(first_ref[1], nodes, NT) + bias_ref[:, :1]
    cot_part = dot(second_ref[...], cot, NT)

    src_high, src_low = split_two(0.5 * src_part)
    dst_high, dst_low = split_two(0.5 * dst_part)
    cot_high, cot_low = split_two((0.5 * scale) * cot_part)
    for i, piece in enumerate([src_high, dst_high, src_low, dst_low]):
        left[:, i * node_total : (i + 1) * node_total] = piece
    left_back[:, :node_total] = cot_high
    left_back[:, node_total:] = cot_low
    total[...] = jnp.zeros_like(total)
    kind = BF16 if quants == 4 else F32
    step = edges.shape[2]
    node_at = lax.broadcasted_iota(jnp.int32, (node_total, step), 0).astype(F32).astype(kind)

    def one_hot(row):
        same = node_at == row.astype(kind)
        return jnp.where(same, jnp.ones((), kind), jnp.zeros((), kind)).astype(BF16)

    def body(k, carry):
        numbers = edges[k]
        if quants == 4:
            src, dst = numbers[0:1], numbers[1:2]
            weight = numbers[2:3] + numbers[3:4]
        else:
            src = numbers[0:1] * DIGIT + numbers[1:2]
            dst = numbers[2:3] * DIGIT + numbers[3:4]
            weight = numbers[4:5] + numbers[5:6] + numbers[6:7]
        src_hot, dst_hot = one_hot(src), one_hot(dst)
        hot = jnp.concatenate([src_hot, dst_hot], 0)
        halved = dot(left[...], jnp.concatenate([hot, hot], 0), NN)
        back = dot(left_back[...], jnp.concatenate([dst_hot, dst_hot], 0), NN) * weight
        tilt = jnp.tanh(halved)
        rise = 1.0 + tilt
        active = (halved * rise) * weight
        d_pre = back * (rise * (1.0 + halved * (1.0 - tilt)))
        high = weight.astype(BF16).astype(F32)
        low = weight - high
        tail = jnp.concatenate([high, low, jnp.zeros((14, step), F32)], 0)
        right = jnp.concatenate(
            [active.astype(BF16), d_pre.astype(BF16), tail.astype(BF16)], 0
        )
        total[...] += dot(right, hot, NT)
        return carry

    lax.fori_loop(0, edges.shape[0], body, 0, unroll=8 if quants == 4 else 1)
    sums_ref[:part] = (scale * total[:part, node_total:]).astype(BF16)
    sums_ref[part : 2 * part] = total[part : 2 * part, :node_total].astype(BF16)
    sums_ref[2 * part :] = total[part : 2 * part, node_total:].astype(BF16)
    envelope = scale * (
        total[2 * part : 2 * part + 1, node_total:]
        + total[2 * part + 1 : 2 * part + 2, node_total:]
    )
    envelope_ref[...] = jnp.broadcast_to(envelope, envelope_ref.shape)


def take_rows(ref, start, rows):
    if rows % 8 == 0:
        return ref[pl.ds(pl.multiple_of(start, 8), rows), :]
    tall = row_window(rows)
    base = start // 8 * 8
    window = ref[pl.ds(pl.multiple_of(base, 8), tall), :]
    return pltpu.roll(window, lax.rem(tall - (start - base), tall), 0)[:rows]


def row_window(rows):
    return -(-rows // 8) * 8 + 8


def grad_kernel(split, count, groups, place_ref, *refs):
    blocks = refs[:split]
    nodes_ref, cot_ref, envelope_ref = refs[split : split + 3]
    outs = refs[split + 3 : split + 3 + groups]
    active_ref, src_ref, dst_ref = refs[split + 3 + groups : split + 6 + groups]
    left, src_sum, dst_sum = refs[split + 6 + groups :]
    graph, group = place_ref[0], place_ref[1]
    features = nodes_ref.shape[1]
    part = blocks[0].shape[0] // 3
    share = 3 * features // (groups * count)

    turned = nodes_ref[...].astype(F32).T
    left[:features] = turned
    left[features : 2 * features] = turned
    slot = lax.rem(graph, split)
    for k in range(split):
        start = pl.multiple_of((slot ^ k) * part, 8)
        block = blocks[k][...].astype(F32)
        left[pl.ds(pl.multiple_of(2 * features + start, 8), part), :] = block[:part]
        src_sum[pl.ds(start, part), :] = block[part : 2 * part]
        dst_sum[pl.ds(start, part), :] = block[2 * part :]

    src_all = src_sum[...].astype(BF16)
    dst_all = dst_sum[...].astype(BF16)
    cot = cot_ref[...]
    active_ref[...] = left[2 * features : 3 * features].astype(BF16)
    src_ref[...] = src_all
    dst_ref[...] = dst_all

    kinds = []
    rows = []
    for k in range(groups):
        start = (count * (group ^ k) + graph) * share
        rows.append(take_rows(left, start, share))
        kinds.append(start + lax.broadcasted_iota(jnp.int32, rows[-1].shape, 0))
    rows = jnp.concatenate(rows, 0)
    kinds = jnp.concatenate(kinds, 0)
    zero = jnp.zeros_like(rows)
    from_src = jnp.where(kinds < features, rows, zero).astype(BF16)
    from_dst = jnp.where((kinds >= features) & (kinds < 2 * features), rows, zero).astype(BF16)
    from_act = jnp.where(kinds >= 2 * features, rows, zero).astype(BF16)
    grads = dot(from_src, src_all, NT) + dot(from_dst, dst_all, NT) + dot(from_act, cot, NN)

    ones = jnp.ones((8, dst_all.shape[1]), BF16)
    bias_pre = dot(ones, dst_all, NT)[:1]
    env_high, env_low = split_two(envelope_ref[...])
    bias_out = (dot(env_high, cot, NN) + dot(env_low, cot, NN))[:1]
    pre_high = bias_pre.astype(BF16).astype(F32)
    out_high = bias_out.astype(BF16).astype(F32)
    tail = outs[0].shape[0] - share
    pad = jnp.zeros((tail - 4, features), F32)
    extra = jnp.concatenate(
        [pre_high, bias_pre - pre_high, out_high, bias_out - out_high, pad], 0
    )
    for k in range(groups):
        full = jnp.concatenate([grads[k * share : (k + 1) * share], extra], 0)
        outs[k][...] = full.astype(outs[k].dtype)


def node_kernel(place_ref, active_ref, src_ref, dst_ref, envelope_ref, first_ref, second_ref,
                bias_ref, nodes_ref, cot_ref, out_ref, grad_ref, wide):
    rows, features = nodes_ref.shape
    node_total = active_ref.shape[1]
    at = pl.ds(pl.multiple_of(place_ref[0] * rows, rows), rows)

    def own(ref):
        wide[...] = ref[...].astype(F32).T
        return wide[at, :].astype(BF16)

    active = own(active_ref)
    src = own(src_ref)
    dst = own(dst_ref)
    env = envelope_ref[...]
    column = jnp.broadcast_to(env[:1], (node_total, node_total)).T
    wide[:, :node_total] = column
    env_own = wide[at, :1]
    summed = dot(active, second_ref[...], NN) + env_own * bias_ref[1:2, :]
    out_ref[...] = (nodes_ref[...].astype(F32) + summed).astype(BF16)
    back = dot(src, first_ref[:features], NT) + dot(dst, first_ref[features:], NT)
    grad_ref[...] = cot_ref[...].astype(F32) + back


def adam_kernel(groups, *refs):
    parts = refs[:groups]
    master_ref, first_ref, second_ref, bias_ref, bias_first_ref, bias_second_ref = refs[
        groups : groups + 6
    ]
    outs = refs[groups + 6 : groups + 12]
    flat = refs[groups + 12]
    features = parts[0].shape[1]
    total = parts[0][...]
    for ref in parts[1:]:
        total = total + ref[...].astype(F32)
    total = total * (1.0 / groups)
    across = features // LANES
    share = flat.shape[0] // across
    for q in range(across):
        flat[pl.ds(q, share, stride=across), :] = total[:share, q * LANES : (q + 1) * LANES]
    results = adam_update(master_ref[...], first_ref[...], second_ref[...], flat[...])
    for ref, value in zip(outs[:3], results):
        ref[...] = value
    pairs = total[share : share + 4]
    bias_grads = jnp.concatenate([pairs[0:1] + pairs[1:2], pairs[2:3] + pairs[3:4]], 0)
    results = adam_update(bias_ref[...], bias_first_ref[...], bias_second_ref[...], bias_grads)
    for ref, value in zip(outs[3:], results):
        ref[...] = value


def swap(value, axis, count, distance):
    return lax.ppermute(value, axis, [(i, i ^ distance) for i in range(count)])


def gather_blocks(value, axis, count, reach):
    blocks = {0: value}
    for k in range(reach - 2, 0, -2):
        blocks[k] = swap(value, axis, count, k)
    for k in range(0, reach, 2):
        blocks[k + 1] = swap(blocks[k], axis, count, 1)
    return [blocks[k] for k in range(reach)]


def smem():
    return pl.BlockSpec(memory_space=pltpu.SMEM)


def call(body, ins, outs, scratch=(), place=None, flops=0, room=24 << 20,
         far=()):
    far = set(far)
    arrays = [
        pltpu.with_memory_space_constraint(a, pltpu.HBM) if i in far else a
        for i, a in enumerate(ins)
    ]
    specs = [
        pl.BlockSpec(memory_space=pltpu.HBM if i in far else pltpu.VMEM)
        for i in range(len(arrays))
    ]
    if place is not None:
        arrays = [place] + arrays
        specs = [smem()] + specs
    moved = sum(a.size * a.dtype.itemsize for a in list(ins) + list(outs))
    return pl.pallas_call(
        body,
        out_shape=tuple(outs),
        in_specs=specs,
        out_specs=tuple([pl.BlockSpec(memory_space=pltpu.VMEM)] * len(outs)),
        scratch_shapes=list(scratch),
        compiler_params=pltpu.CompilerParams(vmem_limit_bytes=room),
        cost_estimate=pl.CostEstimate(flops=flops, bytes_accessed=moved, transcendentals=0),
    )(*arrays)


def shards(
    nodes,
    cotangent,
    sources,
    targets,
    edge_weight,
    w_first,
    w_second,
    biases,
    master,
    moment_first,
    moment_second,
    bias_first,
    bias_second,
):
    features = nodes.shape[2]
    rows = nodes.shape[1]
    edge_count = sources.shape[1]
    scale = 1.0 / math.sqrt(edge_count / rows)
    count = lax.axis_size("graph")
    groups = lax.axis_size("dp")
    node_total = rows * count
    split = min(count, 2)
    part = features // split
    share = master.shape[0] // features
    struct = jax.ShapeDtypeStruct
    graph = lax.axis_index("graph")
    group = lax.axis_index("dp")

    over = max(i * part % LANES for i in range(split))
    wide = min(features, -(-(part + over) // LANES) * LANES)
    tall = min(features, part if part % 16 == 0 else -(-part // 16) * 16 + 16)
    place = jnp.stack([graph, group]).astype(jnp.int32)

    quants = 4 if node_total <= EXACT else 8
    width = features + quants * edge_count // (2 * rows)
    sources_in = [nodes[0], cotangent[0], sources, targets, edge_weight]
    (packed,) = call(
        functools.partial(pack_kernel, quants),
        sources_in,
        [struct((2 * rows, width), BF16)],
        [pltpu.VMEM(a.shape, a.dtype) for a in sources_in]
        + [pltpu.SemaphoreType.DMA((len(sources_in),))],
        far=range(len(sources_in)),
    )
    blocks = gather_blocks(packed, "graph", count, count)
    weights = call(
        functools.partial(weight_kernel, split),
        [w_first, w_second, biases],
        [
            struct((2, part, features), BF16),
            struct((part, features), BF16),
            struct((part, LANES), F32),
        ],
        [
            pltpu.VMEM((2 * features, wide), BF16),
            pltpu.VMEM((tall, features), BF16),
            pltpu.VMEM((2, wide), F32),
            pltpu.VMEM((wide, features), F32),
            pltpu.SemaphoreType.DMA((3,)),
        ],
        place=place,
        far=range(3),
    )
    sums, envelope, all_nodes, all_cot = call(
        functools.partial(edge_kernel, scale, count),
        blocks + list(weights),
        [
            struct((3 * part, node_total), BF16),
            struct((8, node_total), F32),
            struct((node_total, features), BF16),
            struct((node_total, features), BF16),
        ],
        [
            pltpu.VMEM((part, 4 * node_total), BF16),
            pltpu.VMEM((part, 2 * node_total), BF16),
            pltpu.VMEM((count, quants, edge_count), F32),
            pltpu.VMEM((2 * part + 16, 2 * node_total), F32),
        ],
        place=place,
        flops=8 * part * 2 * node_total * edge_count * count,
    )
    blocks = gather_blocks(sums, "graph", count, split)
    tall = -(-(share + 4) // 16) * 16
    results = call(
        functools.partial(grad_kernel, split, count, groups),
        blocks + [all_nodes, all_cot, envelope],
        [struct((tall, features), F32)]
        + [struct((tall, features), BF16)] * (groups - 1)
        + [struct((features, node_total), BF16)] * 3,
        [
            pltpu.VMEM((3 * features + 16, node_total), F32),
            pltpu.VMEM((features, node_total), F32),
            pltpu.VMEM((features, node_total), F32),
        ],
        place=place,
        flops=2 * groups * share * 3 * node_total * features,
    )
    grads = results[:groups]
    active, src_sum, dst_sum = results[groups:]
    received = [grads[0]]
    for k in range(1, groups):
        received.append(swap(grads[k], "dp", groups, k))
    node_out, node_grad = call(
        node_kernel,
        [active, src_sum, dst_sum, envelope, w_first, w_second, biases, nodes[0], cotangent[0]],
        [struct((rows, features), BF16), struct((rows, features), F32)],
        [pltpu.VMEM((node_total, features), F32)],
        place=place,
        flops=6 * node_total * features * features,
    )
    lanes = (share * (features // LANES), LANES)
    updated = call(
        functools.partial(adam_kernel, groups),
        received
        + [master.reshape(lanes), moment_first.reshape(lanes), moment_second.reshape(lanes)]
        + [biases, bias_first, bias_second],
        [struct(lanes, F32)] * 3 + [struct(biases.shape, F32)] * 3,
        [pltpu.VMEM(lanes, F32)],
    )
    return (
        node_out[None],
        node_grad[None],
        updated[0].reshape(master.shape),
        updated[1].reshape(master.shape),
        updated[2].reshape(master.shape),
        updated[3],
        updated[4],
        updated[5],
    )


def solution(mesh):
    placed = (
        P("dp", "graph", None),
        P("dp", "graph", None),
        P("dp", "graph"),
        P("dp", "graph"),
        P("dp", "graph"),
        P(),
        P(),
        P(),
        P(("dp", "graph")),
        P(("dp", "graph")),
        P(("dp", "graph")),
        P(),
        P(),
    )
    return jax.shard_map(
        shards,
        mesh=mesh,
        in_specs=placed,
        out_specs=(
            P("dp", "graph", None),
            P("dp", "graph", None),
            P(("dp", "graph")),
            P(("dp", "graph")),
            P(("dp", "graph")),
            P(),
            P(),
            P(),
        ),
        check_vma=False,
    )
```

```python
import functools
import math

import jax
import jax.numpy as jnp
from jax import lax
from jax.experimental import pallas as pl
from jax.experimental.pallas import tpu as pltpu
from jax.sharding import PartitionSpec as P


STEP = 10

beta_one = 0.9
beta_two = 0.999
epsilon = 1e-08
learn_rate = 0.001

F32 = jnp.float32
BF16 = jnp.bfloat16
LANES = 128
EXACT = 256
DIGIT = 16.0

NN = (((1,), (0,)), ((), ()))
NT = (((1,), (1,)), ((), ()))


def dot(a, b, dims):
    return lax.dot_general(a, b, dims, preferred_element_type=F32)


def split_two(x):
    high = x.astype(BF16)
    low = (x - high.astype(F32)).astype(BF16)
    return high, low


def adam_update(param, first, second, grads):
    new_first = beta_one * first + (1.0 - beta_one) * grads
    new_second = beta_two * second + (1.0 - beta_two) * grads * grads
    ratio = (
        new_first
        / (1.0 - beta_one**STEP)
        / (jnp.sqrt(new_second / (1.0 - beta_two**STEP)) + epsilon)
    )
    return (param - learn_rate * ratio, new_first, new_second)


def pack_kernel(quants, *refs):
    sources, out_ref, held, sems = refs[:5], refs[5], refs[6:11], refs[11]
    copies = [
        pltpu.make_async_copy(source, target, sems.at[i])
        for i, (source, target) in enumerate(zip(sources, held))
    ]
    for copy in copies:
        copy.start()
    for copy in copies:
        copy.wait()
    nodes_ref, cot_ref, src_ref, dst_ref, weight_ref = held
    rows, features = nodes_ref.shape
    width = out_ref.shape[1]
    beside = width - features
    rest = features - beside
    half = width - rest
    out_ref[:rows, :features] = nodes_ref[...]
    out_ref[:rows, features:] = cot_ref[:, :beside]
    out_ref[rows:, :rest] = cot_ref[:, beside:]

    src = src_ref[...].astype(F32)
    dst = dst_ref[...].astype(F32)
    weight = weight_ref[...]
    first = weight.astype(BF16).astype(F32)
    second = (weight - first).astype(BF16).astype(F32)
    if quants == 4:
        values = [src, dst, first, second]
    else:
        src_high = jnp.floor(src * (1.0 / DIGIT))
        dst_high = jnp.floor(dst * (1.0 / DIGIT))
        values = [src_high, src - src_high * DIGIT, dst_high, dst - dst_high * DIGIT]
        values += [first, second, weight - first - second, jnp.zeros_like(first)]
    values = jnp.concatenate(values, 0)
    pieces = rows // quants
    stacked = jnp.concatenate(
        [values[:, i * half : (i + 1) * half] for i in range(pieces)], 0
    )
    out_ref[rows:, rest:] = stacked.astype(BF16)


def weight_kernel(split, place_ref, first_ref, second_ref, bias_ref, *refs):
    targets, sems = refs[:3], refs[3]
    part = targets[1].shape[0]
    mine = pl.ds(pl.multiple_of(lax.rem(place_ref[0], split) * part, LANES), part)
    sources = [first_ref.at[:, mine], second_ref.at[mine, :], bias_ref.at[:, mine]]
    copies = [
        pltpu.make_async_copy(source, target, sems.at[i])
        for i, (source, target) in enumerate(zip(sources, targets))
    ]
    for copy in copies:
        copy.start()
    for copy in copies:
        copy.wait()


def edge_kernel(scale, count, place_ref, *refs):
    blocks = refs[:count]
    first_ref, second_ref, bias_ref = refs[count : count + 3]
    sums_ref, envelope_ref, nodes_ref, cot_ref = refs[count + 3 : count + 7]
    left, left_back, edges, total = refs[count + 7 :]
    graph = place_ref[0]
    features = nodes_ref.shape[1]
    node_total = nodes_ref.shape[0]
    rows = node_total // count
    part = sums_ref.shape[0] // 3
    width = blocks[0].shape[1]
    beside = width - features
    rest = features - beside
    half = width - rest
    quants = edges.shape[1]
    pieces = rows // quants

    for k in range(count):
        at = pl.ds(pl.multiple_of((graph ^ k) * rows, rows), rows)
        nodes_ref[at, :] = blocks[k][:rows, :features]
        cot_ref[at, :beside] = blocks[k][:rows, features:]
        cot_ref[at, beside:] = blocks[k][rows:, :rest]
        numbers = blocks[k][rows:, rest:].astype(F32)
        for i in range(pieces):
            edges[k, :, i * half : (i + 1) * half] = numbers[i * quants : (i + 1) * quants]

    nodes = nodes_ref[...]
    cot = cot_ref[...]
    src_part = dot(nodes, first_ref[:features], NN).T
    dst_part = (dot(nodes, first_ref[features:], NN) + bias_ref[:1, :]).T
    cot_part = dot(second_ref[...], cot, NT)

    cot_high, cot_low = split_two((0.5 * scale) * cot_part)
    left[:, :node_total] = (0.5 * src_part).astype(BF16)
    left[:, node_total:] = (0.5 * dst_part).astype(BF16)
    left_back[:, :node_total] = cot_high
    left_back[:, node_total:] = cot_low
    total[...] = jnp.zeros_like(total)
    kind = BF16 if quants == 4 else F32
    step = edges.shape[2]
    node_at = lax.broadcasted_iota(jnp.int32, (node_total, step), 0).astype(F32).astype(kind)

    def one_hot(row):
        same = node_at == row.astype(kind)
        return jnp.where(same, jnp.ones((), kind), jnp.zeros((), kind)).astype(BF16)

    def body(k, carry):
        numbers = edges[k]
        if quants == 4:
            src, dst = numbers[0:1], numbers[1:2]
            weight = numbers[2:3] + numbers[3:4]
        else:
            src = numbers[0:1] * DIGIT + numbers[1:2]
            dst = numbers[2:3] * DIGIT + numbers[3:4]
            weight = numbers[4:5] + numbers[5:6] + numbers[6:7]
        src_hot, dst_hot = one_hot(src), one_hot(dst)
        hot = jnp.concatenate([src_hot, dst_hot], 0)
        halved = dot(left[...], hot, NN)
        back = dot(left_back[...], jnp.concatenate([dst_hot, dst_hot], 0), NN) * weight
        tilt = jnp.tanh(halved)
        rise = 1.0 + tilt
        active = (halved * rise) * weight
        d_pre = back * (rise * (1.0 + halved * (1.0 - tilt)))
        high = weight.astype(BF16).astype(F32)
        low = weight - high
        tail = jnp.concatenate([high, low, jnp.zeros((14, step), F32)], 0)
        right = jnp.concatenate(
            [active.astype(BF16), d_pre.astype(BF16), tail.astype(BF16)], 0
        )
        total[...] += dot(right, hot, NT)
        return carry

    lax.fori_loop(0, edges.shape[0], body, 0, unroll=8 if quants == 4 else 1)
    sums_ref[:part] = scale * total[:part, node_total:]
    sums_ref[part : 2 * part] = total[part : 2 * part, :node_total]
    sums_ref[2 * part :] = total[part : 2 * part, node_total:]
    envelope = scale * (
        total[2 * part : 2 * part + 1, node_total:]
        + total[2 * part + 1 : 2 * part + 2, node_total:]
    )
    envelope_ref[...] = jnp.broadcast_to(envelope, envelope_ref.shape)


def take_rows(ref, start, rows):
    if rows % 8 == 0:
        return ref[pl.ds(pl.multiple_of(start, 8), rows), :]
    tall = row_window(rows)
    base = start // 8 * 8
    window = ref[pl.ds(pl.multiple_of(base, 8), tall), :]
    return pltpu.roll(window, lax.rem(tall - (start - base), tall), 0)[:rows]


def row_window(rows):
    return -(-rows // 8) * 8 + 8


def grad_kernel(split, count, groups, place_ref, *refs):
    blocks = refs[:split]
    nodes_ref, cot_ref, envelope_ref = refs[split : split + 3]
    outs = refs[split + 3 : split + 3 + groups]
    active_ref, src_ref, dst_ref = refs[split + 3 + groups : split + 6 + groups]
    left, src_sum, dst_sum = refs[split + 6 + groups :]
    graph, group = place_ref[0], place_ref[1]
    features = nodes_ref.shape[1]
    part = blocks[0].shape[0] // 3
    share = 3 * features // (groups * count)

    turned = nodes_ref[...].astype(F32).T
    left[:features] = turned
    left[features : 2 * features] = turned
    slot = lax.rem(graph, split)
    for k in range(split):
        start = pl.multiple_of((slot ^ k) * part, 8)
        block = blocks[k][...]
        left[pl.ds(pl.multiple_of(2 * features + start, 8), part), :] = block[:part]
        src_sum[pl.ds(start, part), :] = block[part : 2 * part]
        dst_sum[pl.ds(start, part), :] = block[2 * part :]

    src_all = jnp.concatenate(split_two(src_sum[...]), 1)
    dst_all = jnp.concatenate(split_two(dst_sum[...]), 1)
    cot = cot_ref[...]
    active_ref[...] = left[2 * features : 3 * features]
    src_ref[...] = src_sum[...]
    dst_ref[...] = dst_sum[...]

    kinds = []
    rows = []
    for k in range(groups):
        start = (count * (group ^ k) + graph) * share
        rows.append(take_rows(left, start, share))
        kinds.append(start + lax.broadcasted_iota(jnp.int32, rows[-1].shape, 0))
    rows = jnp.concatenate(rows, 0)
    kinds = jnp.concatenate(kinds, 0)
    zero = jnp.zeros_like(rows)
    from_src = jnp.where(kinds < features, rows, zero).astype(BF16)
    from_dst = jnp.where((kinds >= features) & (kinds < 2 * features), rows, zero).astype(BF16)
    from_act = jnp.concatenate(split_two(jnp.where(kinds >= 2 * features, rows, zero)), 1)
    grads = (
        dot(jnp.concatenate([from_src, from_src], 1), src_all, NT)
        + dot(jnp.concatenate([from_dst, from_dst], 1), dst_all, NT)
        + dot(from_act, jnp.concatenate([cot, cot], 0), NN)
    )

    ones = jnp.ones((8, dst_all.shape[1]), BF16)
    bias_pre = dot(ones, dst_all, NT)[:1]
    env_high, env_low = split_two(envelope_ref[...])
    bias_out = (dot(env_high, cot, NN) + dot(env_low, cot, NN))[:1]
    pre_high = bias_pre.astype(BF16).astype(F32)
    out_high = bias_out.astype(BF16).astype(F32)
    tail = outs[0].shape[0] - share
    pad = jnp.zeros((tail - 4, features), F32)
    extra = jnp.concatenate(
        [pre_high, bias_pre - pre_high, out_high, bias_out - out_high, pad], 0
    )
    for k in range(groups):
        full = jnp.concatenate([grads[k * share : (k + 1) * share], extra], 0)
        outs[k][...] = full.astype(outs[k].dtype)


def node_kernel(place_ref, active_ref, src_ref, dst_ref, envelope_ref, first_ref, second_ref,
                bias_ref, nodes_ref, cot_ref, out_ref, grad_ref, wide):
    rows, features = nodes_ref.shape
    node_total = active_ref.shape[1]
    at = pl.ds(pl.multiple_of(place_ref[0] * rows, rows), rows)

    def own(ref):
        wide[...] = ref[...].T
        return jnp.concatenate(split_two(wide[at, :]), 0)

    def both(value, weight, dims):
        result = dot(value, weight, dims)
        return result[:rows] + result[rows:]

    active = own(active_ref)
    src = own(src_ref)
    dst = own(dst_ref)
    env = envelope_ref[...]
    column = jnp.broadcast_to(env[:1], (node_total, node_total)).T
    wide[:, :node_total] = column
    env_own = wide[at, :1]
    summed = both(active, second_ref[...], NN) + env_own * bias_ref[1:2, :]
    out_ref[...] = (nodes_ref[...].astype(F32) + summed).astype(BF16)
    back = both(src, first_ref[:features], NT) + both(dst, first_ref[features:], NT)
    grad_ref[...] = cot_ref[...].astype(F32) + back


def adam_kernel(groups, *refs):
    parts = refs[:groups]
    master_ref, first_ref, second_ref, bias_ref, bias_first_ref, bias_second_ref = refs[
        groups : groups + 6
    ]
    outs = refs[groups + 6 : groups + 12]
    flat = refs[groups + 12]
    features = parts[0].shape[1]
    total = parts[0][...]
    for ref in parts[1:]:
        total = total + ref[...].astype(F32)
    total = total * (1.0 / groups)
    across = features // LANES
    share = flat.shape[0] // across
    for q in range(across):
        flat[pl.ds(q, share, stride=across), :] = total[:share, q * LANES : (q + 1) * LANES]
    results = adam_update(master_ref[...], first_ref[...], second_ref[...], flat[...])
    for ref, value in zip(outs[:3], results):
        ref[...] = value
    pairs = total[share : share + 4]
    bias_grads = jnp.concatenate([pairs[0:1] + pairs[1:2], pairs[2:3] + pairs[3:4]], 0)
    results = adam_update(bias_ref[...], bias_first_ref[...], bias_second_ref[...], bias_grads)
    for ref, value in zip(outs[3:], results):
        ref[...] = value


def swap(value, axis, count, distance):
    return lax.ppermute(value, axis, [(i, i ^ distance) for i in range(count)])


def gather_blocks(value, axis, count, reach):
    blocks = {0: value}
    for k in range(reach - 2, 0, -2):
        blocks[k] = swap(value, axis, count, k)
    for k in range(0, reach, 2):
        blocks[k + 1] = swap(blocks[k], axis, count, 1)
    return [blocks[k] for k in range(reach)]


def smem():
    return pl.BlockSpec(memory_space=pltpu.SMEM)


def call(body, ins, outs, scratch=(), place=None, flops=0, room=24 << 20,
         far=()):
    far = set(far)
    arrays = [
        pltpu.with_memory_space_constraint(a, pltpu.HBM) if i in far else a
        for i, a in enumerate(ins)
    ]
    specs = [
        pl.BlockSpec(memory_space=pltpu.HBM if i in far else pltpu.VMEM)
        for i in range(len(arrays))
    ]
    if place is not None:
        arrays = [place] + arrays
        specs = [smem()] + specs
    moved = sum(a.size * a.dtype.itemsize for a in list(ins) + list(outs))
    return pl.pallas_call(
        body,
        out_shape=tuple(outs),
        in_specs=specs,
        out_specs=tuple([pl.BlockSpec(memory_space=pltpu.VMEM)] * len(outs)),
        scratch_shapes=list(scratch),
        compiler_params=pltpu.CompilerParams(vmem_limit_bytes=room),
        cost_estimate=pl.CostEstimate(flops=flops, bytes_accessed=moved, transcendentals=0),
    )(*arrays)


def shards(
    nodes,
    cotangent,
    sources,
    targets,
    edge_weight,
    w_first,
    w_second,
    biases,
    master,
    moment_first,
    moment_second,
    bias_first,
    bias_second,
):
    features = nodes.shape[2]
    rows = nodes.shape[1]
    edge_count = sources.shape[1]
    scale = 1.0 / math.sqrt(edge_count / rows)
    count = lax.axis_size("graph")
    groups = lax.axis_size("dp")
    node_total = rows * count
    split = min(count, 2)
    part = features // split
    share = master.shape[0] // features
    struct = jax.ShapeDtypeStruct
    graph = lax.axis_index("graph")
    group = lax.axis_index("dp")

    place = jnp.stack([graph, group]).astype(jnp.int32)

    quants = 4 if node_total <= EXACT else 8
    width = features + quants * edge_count // (2 * rows)
    sources_in = [nodes[0], cotangent[0], sources, targets, edge_weight]
    (packed,) = call(
        functools.partial(pack_kernel, quants),
        sources_in,
        [struct((2 * rows, width), BF16)],
        [pltpu.VMEM(a.shape, a.dtype) for a in sources_in]
        + [pltpu.SemaphoreType.DMA((len(sources_in),))],
        far=range(len(sources_in)),
    )
    blocks = gather_blocks(packed, "graph", count, count)
    weights = call(
        functools.partial(weight_kernel, split),
        [w_first, w_second, biases],
        [
            struct((2 * features, part), BF16),
            struct((part, features), BF16),
            struct((2, part), F32),
        ],
        [pltpu.SemaphoreType.DMA((3,))],
        place=place,
        far=range(3),
    )
    sums, envelope, all_nodes, all_cot = call(
        functools.partial(edge_kernel, scale, count),
        blocks + list(weights),
        [
            struct((3 * part, node_total), F32),
            struct((8, node_total), F32),
            struct((node_total, features), BF16),
            struct((node_total, features), BF16),
        ],
        [
            pltpu.VMEM((part, 2 * node_total), BF16),
            pltpu.VMEM((part, 2 * node_total), BF16),
            pltpu.VMEM((count, quants, edge_count), F32),
            pltpu.VMEM((2 * part + 16, 2 * node_total), F32),
        ],
        place=place,
        flops=8 * part * 2 * node_total * edge_count * count,
    )
    blocks = gather_blocks(sums, "graph", count, split)
    tall = -(-(share + 4) // 16) * 16
    results = call(
        functools.partial(grad_kernel, split, count, groups),
        blocks + [all_nodes, all_cot, envelope],
        [struct((tall, features), F32)]
        + [struct((tall, features), BF16)] * (groups - 1)
        + [struct((features, node_total), F32)] * 3,
        [
            pltpu.VMEM((3 * features + 16, node_total), F32),
            pltpu.VMEM((features, node_total), F32),
            pltpu.VMEM((features, node_total), F32),
        ],
        place=place,
        flops=2 * groups * share * 3 * node_total * features,
    )
    grads = results[:groups]
    active, src_sum, dst_sum = results[groups:]
    received = [grads[0]]
    for k in range(1, groups):
        received.append(swap(grads[k], "dp", groups, k))
    node_out, node_grad = call(
        node_kernel,
        [active, src_sum, dst_sum, envelope, w_first, w_second, biases, nodes[0], cotangent[0]],
        [struct((rows, features), BF16), struct((rows, features), F32)],
        [pltpu.VMEM((node_total, features), F32)],
        place=place,
        flops=6 * node_total * features * features,
    )
    lanes = (share * (features // LANES), LANES)
    updated = call(
        functools.partial(adam_kernel, groups),
        received
        + [master.reshape(lanes), moment_first.reshape(lanes), moment_second.reshape(lanes)]
        + [biases, bias_first, bias_second],
        [struct(lanes, F32)] * 3 + [struct(biases.shape, F32)] * 3,
        [pltpu.VMEM(lanes, F32)],
    )
    return (
        node_out[None],
        node_grad[None],
        updated[0].reshape(master.shape),
        updated[1].reshape(master.shape),
        updated[2].reshape(master.shape),
        updated[3],
        updated[4],
        updated[5],
    )


def solution(mesh):
    placed = (
        P("dp", "graph", None),
        P("dp", "graph", None),
        P("dp", "graph"),
        P("dp", "graph"),
        P("dp", "graph"),
        P(),
        P(),
        P(),
        P(("dp", "graph")),
        P(("dp", "graph")),
        P(("dp", "graph")),
        P(),
        P(),
    )
    return jax.shard_map(
        shards,
        mesh=mesh,
        in_specs=placed,
        out_specs=(
            P("dp", "graph", None),
            P("dp", "graph", None),
            P(("dp", "graph")),
            P(("dp", "graph")),
            P(("dp", "graph")),
            P(),
            P(),
            P(),
        ),
        check_vma=False,
    )
```

```python
import functools
import math

import jax
import jax.numpy as jnp
from jax import lax
from jax.experimental import pallas as pl
from jax.experimental.pallas import tpu as pltpu
from jax.sharding import PartitionSpec as P


STEP = 10

beta_one = 0.9
beta_two = 0.999
epsilon = 1e-08
learn_rate = 0.001

F32 = jnp.float32
BF16 = jnp.bfloat16
LANES = 128
EXACT = 256
DIGIT = 16.0

NN = (((1,), (0,)), ((), ()))
NT = (((1,), (1,)), ((), ()))


def dot(a, b, dims):
    return lax.dot_general(a, b, dims, preferred_element_type=F32)


def split_two(x):
    high = x.astype(BF16)
    low = (x - high.astype(F32)).astype(BF16)
    return high, low


def adam_update(param, first, second, grads):
    new_first = beta_one * first + (1.0 - beta_one) * grads
    new_second = beta_two * second + (1.0 - beta_two) * grads * grads
    ratio = (
        new_first
        / (1.0 - beta_one**STEP)
        / (jnp.sqrt(new_second / (1.0 - beta_two**STEP)) + epsilon)
    )
    return (param - learn_rate * ratio, new_first, new_second)


def pack_kernel(quants, *refs):
    sources, out_ref, held, sems = refs[:5], refs[5], refs[6:11], refs[11]
    copies = [
        pltpu.make_async_copy(source, target, sems.at[i])
        for i, (source, target) in enumerate(zip(sources, held))
    ]
    for copy in copies:
        copy.start()
    for copy in copies:
        copy.wait()
    nodes_ref, cot_ref, src_ref, dst_ref, weight_ref = held
    rows, features = nodes_ref.shape
    width = out_ref.shape[1]
    beside = width - features
    rest = features - beside
    half = width - rest
    out_ref[:rows, :features] = nodes_ref[...]
    out_ref[:rows, features:] = cot_ref[:, :beside]
    out_ref[rows:, :rest] = cot_ref[:, beside:]

    src = src_ref[...].astype(F32)
    dst = dst_ref[...].astype(F32)
    weight = weight_ref[...]
    first = weight.astype(BF16).astype(F32)
    second = (weight - first).astype(BF16).astype(F32)
    if quants == 4:
        values = [src, dst, first, second]
    else:
        src_high = jnp.floor(src * (1.0 / DIGIT))
        dst_high = jnp.floor(dst * (1.0 / DIGIT))
        values = [src_high, src - src_high * DIGIT, dst_high, dst - dst_high * DIGIT]
        values += [first, second, weight - first - second, jnp.zeros_like(first)]
    values = jnp.concatenate(values, 0)
    pieces = rows // quants
    stacked = jnp.concatenate(
        [values[:, i * half : (i + 1) * half] for i in range(pieces)], 0
    )
    out_ref[rows:, rest:] = stacked.astype(BF16)


def weight_kernel(split, place_ref, first_ref, second_ref, bias_ref, *refs):
    targets, sems = refs[:3], refs[3]
    part = targets[1].shape[0]
    mine = pl.ds(pl.multiple_of(lax.rem(place_ref[0], split) * part, LANES), part)
    sources = [first_ref.at[:, mine], second_ref.at[mine, :], bias_ref.at[:, mine]]
    copies = [
        pltpu.make_async_copy(source, target, sems.at[i])
        for i, (source, target) in enumerate(zip(sources, targets))
    ]
    for copy in copies:
        copy.start()
    for copy in copies:
        copy.wait()


def edge_kernel(scale, count, place_ref, *refs):
    blocks = refs[:count]
    first_ref, second_ref, bias_ref = refs[count : count + 3]
    sums_ref, envelope_ref, nodes_ref, cot_ref = refs[count + 3 : count + 7]
    left, left_back, edges, total = refs[count + 7 :]
    graph = place_ref[0]
    features = nodes_ref.shape[1]
    node_total = nodes_ref.shape[0]
    rows = node_total // count
    part = sums_ref.shape[0] // 3
    width = blocks[0].shape[1]
    beside = width - features
    rest = features - beside
    half = width - rest
    quants = edges.shape[1]
    pieces = rows // quants

    for k in range(count):
        at = pl.ds(pl.multiple_of((graph ^ k) * rows, rows), rows)
        nodes_ref[at, :] = blocks[k][:rows, :features]
        cot_ref[at, :beside] = blocks[k][:rows, features:]
        cot_ref[at, beside:] = blocks[k][rows:, :rest]
        numbers = blocks[k][rows:, rest:].astype(F32)
        for i in range(pieces):
            edges[graph ^ k, :, i * half : (i + 1) * half] = numbers[i * quants : (i + 1) * quants]

    nodes = nodes_ref[...]
    cot = cot_ref[...]
    src_part = dot(nodes, first_ref[:features], NN).T
    dst_part = (dot(nodes, first_ref[features:], NN) + bias_ref[:1, :]).T
    cot_part = dot(second_ref[...], cot, NT)

    cot_high, cot_low = split_two((0.5 * scale) * cot_part)
    left[:, :node_total] = (0.5 * src_part).astype(BF16)
    left[:, node_total:] = (0.5 * dst_part).astype(BF16)
    left_back[:, :node_total] = cot_high
    left_back[:, node_total:] = cot_low
    total[...] = jnp.zeros_like(total)
    kind = BF16 if quants == 4 else F32
    step = edges.shape[2]
    node_at = lax.broadcasted_iota(jnp.int32, (node_total, step), 0).astype(F32).astype(kind)

    def one_hot(row):
        same = node_at == row.astype(kind)
        return jnp.where(same, jnp.ones((), kind), jnp.zeros((), kind)).astype(BF16)

    def body(k, carry):
        numbers = edges[k]
        if quants == 4:
            src, dst = numbers[0:1], numbers[1:2]
            weight = numbers[2:3] + numbers[3:4]
        else:
            src = numbers[0:1] * DIGIT + numbers[1:2]
            dst = numbers[2:3] * DIGIT + numbers[3:4]
            weight = numbers[4:5] + numbers[5:6] + numbers[6:7]
        src_hot, dst_hot = one_hot(src), one_hot(dst)
        hot = jnp.concatenate([src_hot, dst_hot], 0)
        halved = dot(left[...], hot, NN)
        back = dot(left_back[...], jnp.concatenate([dst_hot, dst_hot], 0), NN) * weight
        tilt = jnp.tanh(halved)
        rise = 1.0 + tilt
        active = (halved * rise) * weight
        d_pre = back * (rise * (1.0 + halved * (1.0 - tilt)))
        high = weight.astype(BF16).astype(F32)
        low = weight - high
        tail = jnp.concatenate([high, low, jnp.zeros((14, step), F32)], 0)
        right = jnp.concatenate(
            [active.astype(BF16), d_pre.astype(BF16), tail.astype(BF16)], 0
        )
        total[...] += dot(right, hot, NT)
        return carry

    lax.fori_loop(0, edges.shape[0], body, 0, unroll=8 if quants == 4 else 1)
    sums_ref[:part] = scale * total[:part, node_total:]
    sums_ref[part : 2 * part] = total[part : 2 * part, :node_total]
    sums_ref[2 * part :] = total[part : 2 * part, node_total:]
    envelope = scale * (
        total[2 * part : 2 * part + 1, node_total:]
        + total[2 * part + 1 : 2 * part + 2, node_total:]
    )
    envelope_ref[...] = jnp.broadcast_to(envelope, envelope_ref.shape)


def take_rows(ref, start, rows):
    if rows % 8 == 0:
        return ref[pl.ds(pl.multiple_of(start, 8), rows), :]
    tall = row_window(rows)
    base = start // 8 * 8
    window = ref[pl.ds(pl.multiple_of(base, 8), tall), :]
    return pltpu.roll(window, lax.rem(tall - (start - base), tall), 0)[:rows]


def row_window(rows):
    return -(-rows // 8) * 8 + 8


def grad_kernel(split, count, groups, place_ref, *refs):
    blocks = refs[:split]
    nodes_ref, cot_ref, envelope_ref = refs[split : split + 3]
    outs = refs[split + 3 : split + 3 + groups]
    active_ref, src_ref, dst_ref = refs[split + 3 + groups : split + 6 + groups]
    left, src_sum, dst_sum = refs[split + 6 + groups :]
    graph, group = place_ref[0], place_ref[1]
    features = nodes_ref.shape[1]
    part = blocks[0].shape[0] // 3
    share = 3 * features // (groups * count)

    turned = nodes_ref[...].astype(F32).T
    left[:features] = turned
    left[features : 2 * features] = turned
    slot = lax.rem(graph, split)
    for k in range(split):
        start = pl.multiple_of((slot ^ k) * part, 8)
        block = blocks[k][...]
        left[pl.ds(pl.multiple_of(2 * features + start, 8), part), :] = block[:part]
        src_sum[pl.ds(start, part), :] = block[part : 2 * part]
        dst_sum[pl.ds(start, part), :] = block[2 * part :]

    src_all = jnp.concatenate(split_two(src_sum[...]), 1)
    dst_all = jnp.concatenate(split_two(dst_sum[...]), 1)
    cot = cot_ref[...]
    active_ref[...] = left[2 * features : 3 * features]
    src_ref[...] = src_sum[...]
    dst_ref[...] = dst_sum[...]

    kinds = []
    rows = []
    for k in range(groups):
        start = (count * (group ^ k) + graph) * share
        rows.append(take_rows(left, start, share))
        kinds.append(start + lax.broadcasted_iota(jnp.int32, rows[-1].shape, 0))
    rows = jnp.concatenate(rows, 0)
    kinds = jnp.concatenate(kinds, 0)
    zero = jnp.zeros_like(rows)
    from_src = jnp.where(kinds < features, rows, zero).astype(BF16)
    from_dst = jnp.where((kinds >= features) & (kinds < 2 * features), rows, zero).astype(BF16)
    from_act = jnp.concatenate(split_two(jnp.where(kinds >= 2 * features, rows, zero)), 1)
    grads = (
        dot(jnp.concatenate([from_src, from_src], 1), src_all, NT)
        + dot(jnp.concatenate([from_dst, from_dst], 1), dst_all, NT)
        + dot(from_act, jnp.concatenate([cot, cot], 0), NN)
    )

    ones = jnp.ones((8, dst_all.shape[1]), BF16)
    bias_pre = dot(ones, dst_all, NT)[:1]
    env_high, env_low = split_two(envelope_ref[...])
    bias_out = (dot(env_high, cot, NN) + dot(env_low, cot, NN))[:1]
    pre_high, pre_low = [piece.astype(F32) for piece in split_two(bias_pre)]
    out_high, out_low = [piece.astype(F32) for piece in split_two(bias_out)]
    tail = outs[0].shape[0] - share
    pad = jnp.zeros((tail - 4, features), F32)
    extra = jnp.concatenate(
        [pre_high, pre_low, out_high, out_low, pad], 0
    )
    for k in range(groups):
        full = jnp.concatenate([grads[k * share : (k + 1) * share], extra], 0)
        outs[k][...] = full.astype(outs[k].dtype)


def node_kernel(place_ref, active_ref, src_ref, dst_ref, envelope_ref, first_ref, second_ref,
                bias_ref, nodes_ref, cot_ref, out_ref, grad_ref, wide):
    rows, features = nodes_ref.shape
    node_total = active_ref.shape[1]
    at = pl.ds(pl.multiple_of(place_ref[0] * rows, rows), rows)

    def own(ref):
        wide[...] = ref[...].T
        return jnp.concatenate(split_two(wide[at, :]), 0)

    def both(value, weight, dims):
        result = dot(value, weight, dims)
        return result[:rows] + result[rows:]

    active = own(active_ref)
    src = own(src_ref)
    dst = own(dst_ref)
    env = envelope_ref[...]
    column = jnp.broadcast_to(env[:1], (node_total, node_total)).T
    wide[:, :node_total] = column
    env_own = wide[at, :1]
    summed = both(active, second_ref[...], NN) + env_own * bias_ref[1:2, :]
    out_ref[...] = (nodes_ref[...].astype(F32) + summed).astype(BF16)
    back = both(src, first_ref[:features], NT) + both(dst, first_ref[features:], NT)
    grad_ref[...] = cot_ref[...].astype(F32) + back


def adam_kernel(groups, *refs):
    parts = refs[:groups]
    master_ref, first_ref, second_ref, bias_ref, bias_first_ref, bias_second_ref = refs[
        groups : groups + 6
    ]
    outs = refs[groups + 6 : groups + 12]
    flat = refs[groups + 12]
    features = parts[0].shape[1]
    sums = [ref[...].astype(F32) for ref in parts]
    while len(sums) > 1:
        sums = [a + b for a, b in zip(sums[::2], sums[1::2])]
    total = sums[0] * (1.0 / groups)
    across = features // LANES
    share = flat.shape[0] // across
    for q in range(across):
        flat[pl.ds(q, share, stride=across), :] = total[:share, q * LANES : (q + 1) * LANES]
    results = adam_update(master_ref[...], first_ref[...], second_ref[...], flat[...])
    for ref, value in zip(outs[:3], results):
        ref[...] = value
    pairs = total[share : share + 4]
    bias_grads = jnp.concatenate([pairs[0:1] + pairs[1:2], pairs[2:3] + pairs[3:4]], 0)
    results = adam_update(bias_ref[...], bias_first_ref[...], bias_second_ref[...], bias_grads)
    for ref, value in zip(outs[3:], results):
        ref[...] = value


def swap(value, axis, count, distance):
    return lax.ppermute(value, axis, [(i, i ^ distance) for i in range(count)])


def gather_blocks(value, axis, count, reach):
    blocks = {0: value}
    for k in range(reach - 2, 0, -2):
        blocks[k] = swap(value, axis, count, k)
    for k in range(0, reach, 2):
        blocks[k + 1] = swap(blocks[k], axis, count, 1)
    return [blocks[k] for k in range(reach)]


def smem():
    return pl.BlockSpec(memory_space=pltpu.SMEM)


def call(body, ins, outs, scratch=(), place=None, flops=0, room=24 << 20,
         far=()):
    far = set(far)
    arrays = [
        pltpu.with_memory_space_constraint(a, pltpu.HBM) if i in far else a
        for i, a in enumerate(ins)
    ]
    specs = [
        pl.BlockSpec(memory_space=pltpu.HBM if i in far else pltpu.VMEM)
        for i in range(len(arrays))
    ]
    if place is not None:
        arrays = [place] + arrays
        specs = [smem()] + specs
    moved = sum(a.size * a.dtype.itemsize for a in list(ins) + list(outs))
    return pl.pallas_call(
        body,
        out_shape=tuple(outs),
        in_specs=specs,
        out_specs=tuple([pl.BlockSpec(memory_space=pltpu.VMEM)] * len(outs)),
        scratch_shapes=list(scratch),
        compiler_params=pltpu.CompilerParams(vmem_limit_bytes=room),
        cost_estimate=pl.CostEstimate(flops=flops, bytes_accessed=moved, transcendentals=0),
    )(*arrays)


def shards(
    nodes,
    cotangent,
    sources,
    targets,
    edge_weight,
    w_first,
    w_second,
    biases,
    master,
    moment_first,
    moment_second,
    bias_first,
    bias_second,
):
    features = nodes.shape[2]
    rows = nodes.shape[1]
    edge_count = sources.shape[1]
    scale = 1.0 / math.sqrt(edge_count / rows)
    count = lax.axis_size("graph")
    groups = lax.axis_size("dp")
    node_total = rows * count
    split = min(count, 2)
    part = features // split
    share = master.shape[0] // features
    struct = jax.ShapeDtypeStruct
    graph = lax.axis_index("graph")
    group = lax.axis_index("dp")

    place = jnp.stack([graph, group]).astype(jnp.int32)

    quants = 4 if node_total <= EXACT else 8
    width = features + quants * edge_count // (2 * rows)
    sources_in = [nodes[0], cotangent[0], sources, targets, edge_weight]
    (packed,) = call(
        functools.partial(pack_kernel, quants),
        sources_in,
        [struct((2 * rows, width), BF16)],
        [pltpu.VMEM(a.shape, a.dtype) for a in sources_in]
        + [pltpu.SemaphoreType.DMA((len(sources_in),))],
        far=range(len(sources_in)),
    )
    blocks = gather_blocks(packed, "graph", count, count)
    weights = call(
        functools.partial(weight_kernel, split),
        [w_first, w_second, biases],
        [
            struct((2 * features, part), BF16),
            struct((part, features), BF16),
            struct((2, part), F32),
        ],
        [pltpu.SemaphoreType.DMA((3,))],
        place=place,
        far=range(3),
    )
    sums, envelope, all_nodes, all_cot = call(
        functools.partial(edge_kernel, scale, count),
        blocks + list(weights),
        [
            struct((3 * part, node_total), F32),
            struct((8, node_total), F32),
            struct((node_total, features), BF16),
            struct((node_total, features), BF16),
        ],
        [
            pltpu.VMEM((part, 2 * node_total), BF16),
            pltpu.VMEM((part, 2 * node_total), BF16),
            pltpu.VMEM((count, quants, edge_count), F32),
            pltpu.VMEM((2 * part + 16, 2 * node_total), F32),
        ],
        place=place,
        flops=8 * part * 2 * node_total * edge_count * count,
    )
    blocks = gather_blocks(sums, "graph", count, split)
    tall = -(-(share + 4) // 16) * 16
    results = call(
        functools.partial(grad_kernel, split, count, groups),
        blocks + [all_nodes, all_cot, envelope],
        [struct((tall, features), F32)]
        + [struct((tall, features), BF16)] * (groups - 1)
        + [struct((features, node_total), F32)] * 3,
        [
            pltpu.VMEM((3 * features + 16, node_total), F32),
            pltpu.VMEM((features, node_total), F32),
            pltpu.VMEM((features, node_total), F32),
        ],
        place=place,
        flops=2 * groups * share * 3 * node_total * features,
    )
    grads = results[:groups]
    active, src_sum, dst_sum = results[groups:]
    received = [grads[0]]
    for k in range(1, groups):
        received.append(swap(grads[k], "dp", groups, k))
    node_out, node_grad = call(
        node_kernel,
        [active, src_sum, dst_sum, envelope, w_first, w_second, biases, nodes[0], cotangent[0]],
        [struct((rows, features), BF16), struct((rows, features), F32)],
        [pltpu.VMEM((node_total, features), F32)],
        place=place,
        flops=6 * node_total * features * features,
    )
    lanes = (share * (features // LANES), LANES)
    updated = call(
        functools.partial(adam_kernel, groups),
        received
        + [master.reshape(lanes), moment_first.reshape(lanes), moment_second.reshape(lanes)]
        + [biases, bias_first, bias_second],
        [struct(lanes, F32)] * 3 + [struct(biases.shape, F32)] * 3,
        [pltpu.VMEM(lanes, F32)],
    )
    return (
        node_out[None],
        node_grad[None],
        updated[0].reshape(master.shape),
        updated[1].reshape(master.shape),
        updated[2].reshape(master.shape),
        updated[3],
        updated[4],
        updated[5],
    )


def solution(mesh):
    placed = (
        P("dp", "graph", None),
        P("dp", "graph", None),
        P("dp", "graph"),
        P("dp", "graph"),
        P("dp", "graph"),
        P(),
        P(),
        P(),
        P(("dp", "graph")),
        P(("dp", "graph")),
        P(("dp", "graph")),
        P(),
        P(),
    )
    return jax.shard_map(
        shards,
        mesh=mesh,
        in_specs=placed,
        out_specs=(
            P("dp", "graph", None),
            P("dp", "graph", None),
            P(("dp", "graph")),
            P(("dp", "graph")),
            P(("dp", "graph")),
            P(),
            P(),
            P(),
        ),
        check_vma=False,
    )
```
